512 devices in a mesh: wide: 64 (over y_hi, z, x), narrow: 8 (over y_lo, core).
Axes of the slice: x: 4, y: 8 (y_hi: 2, y_lo: 4; y = y_hi * 4 + y_lo), z: 8, core: 2. Of those that a mesh axis runs over, the one named last changes fastest.
Arguments:
- wavefunction: float32 [33554432], P(('wide', 'narrow')), may hold values from -6 to 6
- propagator: float32 [705432], replicated, may hold values from -2.5 to 3.5, as said below
- gate_orders: int32 [6, 11], replicated, may hold values from 0 to 10, each once within a row
- sector_order: int32 [2048], replicated, may hold values from 0 to 2047, as said below
- bond_level: int32 [24], replicated, may hold values from -3 to 3
Outputs:
- evolved: float32 [33554432], P(('wide', 'narrow'))
The draws below stay inside these ranges and needn't reach their ends.
Inputs may be any that keep to these rules, and one draw needn't show every extreme that they name: `propagator`: sector blocks for k = 0 .. 11 set bits, each row-major, one after another in increasing k. `sector_order`: a permutation of 0 .. 2047 listing states with fewer set bits first.
All inputs are finite; a program needn't handle non-finite values.
Results may differ from the reference program's by a relative error of at most 0.0001.
Values sent between devices are 32-bit elements; how exact they have to be, the bound alone decides.
No kernel may reach another device: no remote copies, remote signals or barrier semaphores. Data moves between devices by JAX's collectives and lax.ppermute only.
A program may use at most 64 MiB of HBM per device.

```python
import math
import jax
import jax.numpy as jnp
from jax import lax

LB = 16
GS = 11
GATES = 6
SITES = 25
AMPS = 33554432
STATES = 2048
N_WIDE = 64
N_NARROW = 8


def draw_propagator(key, part):
    blocks_list = []
    for degree in range(GS + 1):
        sector_size = math.comb(GS, degree)
        sub_key = jax.random.fold_in(key, degree + 17)
        entries = jnp.clip(jax.random.normal(sub_key, (sector_size, sector_size), jnp.float32), -4.0, 4.0)
        symmetric = 0.3 * (entries + entries.T) / math.sqrt(sector_size)
        blocks_list.append((jnp.eye(sector_size, dtype=jnp.float32) + symmetric).reshape(-1))
    return jnp.concatenate(blocks_list)


def draw_sector_order(key, part):
    states = jnp.arange(STATES, dtype=jnp.int32)
    weight = jnp.zeros_like(states)
    for position in range(GS):
        weight = weight + (jnp.right_shift(states, position) & 1)
    shuffle = jax.random.permutation(jax.random.fold_in(key, 5), STATES).astype(jnp.int32)
    scores = weight * STATES + shuffle
    return jnp.argsort(scores, stable=True).astype(jnp.int32)


def with_ends(array, stream_key, smallest, high):
    spot = [jax.random.randint(jax.random.fold_in(stream_key, axis), (), 0, length) for axis, length in enumerate(array.shape)]
    widest = array.shape.index(max(array.shape))
    neighbour = spot[:widest] + [(spot[widest] + 1) % array.shape[widest]] + spot[widest + 1:]
    return array.at[tuple(spot)].set(smallest).at[tuple(neighbour)].set(high)


def block_scale(rng, dims, shards, smallest, largest):
    gain, own = 1.0, jax.random.fold_in(rng, 6)
    for dim, shards_of in shards:
        steps = jnp.exp(jax.random.uniform(jax.random.fold_in(own, dim), (shards_of,), jnp.float32, smallest / len(shards), largest / len(shards)))
        gain = gain * jnp.repeat(steps, dims[dim] // shards_of).reshape([-1 if axis == dim else 1 for axis in range(len(dims))])
    return gain


def centred(key, extent, deviation, bound, shards=(), held_as=jnp.bfloat16):
    result = deviation * jax.random.normal(key, extent, jnp.float32)
    if shards:
        result = result * block_scale(key, extent, shards, -0.22, 0.18)
    return jnp.clip(result, -bound, bound).astype(held_as)


def setup_inputs(seed: int = 0) -> dict:
    key_list = jax.random.split(jax.random.key(seed), 6)
    return {
        "wavefunction": centred(key_list[0], (AMPS,), 1.0, 6.0, ((0, 512),), jnp.float32),
        "propagator": draw_propagator(jax.random.fold_in(key_list[5], 71), 0),
        "gate_orders": jax.vmap(lambda own: jax.random.permutation(own, GS))(jax.random.split(key_list[2], GATES)).reshape((GATES, GS)).astype(jnp.int32),
        "sector_order": draw_sector_order(jax.random.fold_in(key_list[5], 71), 0),
        "bond_level": with_ends(jax.random.randint(key_list[4], (SITES - 1,), -3, 4), jax.random.fold_in(key_list[4], 1), -3, 3).astype(jnp.int32),
    }


ZZ_RATE = 0.06
HIGHEST = lax.Precision.HIGHEST


def spin_sign(index_vals, position):
    return 1 - 2 * (jnp.right_shift(index_vals, position) & 1)


def chain_energy(index_vals, levels):
    energy = jnp.zeros(index_vals.shape, jnp.float32)
    for position in range(levels.shape[0]):
        coupled = levels[position] * spin_sign(index_vals, position) * spin_sign(index_vals, position + 1)
        energy = energy + coupled.astype(jnp.float32)
    return energy


def basis_map(gate_row, sector_order):
    mapped = jnp.zeros_like(sector_order)
    for position in range(GS):
        chosen = jnp.right_shift(sector_order, position) & 1
        mapped = mapped + jnp.left_shift(chosen, gate_row[position])
    mapped = mapped.astype(jnp.int32)
    inverse = jnp.argsort(mapped).astype(jnp.int32)
    return mapped, inverse


def sector_blocks(propagator):
    matrices = []
    prop_start = 0
    for degree in range(GS + 1):
        sector_size = math.comb(GS, degree)
        matrices.append(propagator[prop_start:prop_start + sector_size * sector_size].reshape(sector_size, sector_size))
        prop_start += sector_size * sector_size
    return matrices


def apply_middle(amplitudes, maps, matrices):
    mapped, inverse = maps
    packed = jnp.take(amplitudes, mapped, axis=1)
    pieces = []
    row_start = 0
    for matrix in matrices:
        sector_size = matrix.shape[0]
        segment = packed[:, row_start:row_start + sector_size, :]
        pieces.append(jnp.einsum("ij,bjr->bir", matrix, segment, precision=HIGHEST))
        row_start += sector_size
    return jnp.take(jnp.concatenate(pieces, axis=1), inverse, axis=1)


def apply_last(amplitudes, maps, matrices):
    mapped, inverse = maps
    packed = jnp.take(amplitudes, mapped, axis=1)
    pieces = []
    row_start = 0
    for matrix in matrices:
        sector_size = matrix.shape[0]
        segment = packed[:, row_start:row_start + sector_size]
        pieces.append(jnp.einsum("ij,bj->bi", matrix, segment, precision=HIGHEST))
        row_start += sector_size
    return jnp.take(jnp.concatenate(pieces, axis=1), inverse, axis=1)


def reference(wavefunction, propagator, gate_orders, sector_order, bond_level):
    local_size = 2 ** LB
    high_size = AMPS // local_size
    window = 2 ** GS
    lower_size = local_size // window
    left_size = window // (N_NARROW * N_WIDE)
    matrices = sector_blocks(propagator)
    maps = [basis_map(gate_orders[gate_number], sector_order) for gate_number in range(GATES)]
    low_index = jnp.arange(local_size, dtype=jnp.int32)
    high_index = jnp.arange(high_size, dtype=jnp.int32)
    boundary = bond_level[LB - 1] * spin_sign(low_index, LB - 1)
    energy = chain_energy(high_index, bond_level[LB:])[:, None] + chain_energy(low_index, bond_level[:LB - 1])[None, :]
    energy = energy + (spin_sign(high_index, 0)[:, None] * boundary[None, :]).astype(jnp.float32)
    amplitudes = wavefunction.reshape(high_size, local_size) * jnp.exp(-ZZ_RATE * energy)

    def top_gate(values, gate_maps):
        return apply_middle(values.reshape(high_size, window, lower_size), gate_maps, matrices).reshape(high_size, local_size)

    def low_gate(values, gate_maps):
        return apply_last(values.reshape(-1, window), gate_maps, matrices).reshape(high_size, local_size)

    amplitudes = top_gate(amplitudes, maps[0])
    amplitudes = low_gate(amplitudes, maps[1])
    shaped = amplitudes.reshape(N_WIDE, N_NARROW, N_NARROW, N_WIDE, left_size, lower_size)
    moved = jnp.transpose(shaped, (2, 3, 1, 0, 4, 5)).reshape(N_NARROW * N_WIDE, window, lower_size)
    mixed = apply_middle(moved, maps[2], matrices)
    restored = jnp.transpose(mixed.reshape(N_NARROW, N_WIDE, N_NARROW, N_WIDE, left_size, lower_size), (3, 2, 0, 1, 4, 5))
    amplitudes = restored.reshape(high_size, local_size)
    amplitudes = low_gate(amplitudes, maps[3])
    amplitudes = top_gate(amplitudes, maps[4])
    amplitudes = low_gate(amplitudes, maps[5])
    return amplitudes.reshape(-1)
```

```python
import math

import jax
import jax.numpy as jnp
from jax import lax
from jax.experimental import pallas as pl
from jax.experimental.pallas import tpu as pltpu
from jax.sharding import PartitionSpec as P

LB = 16
GS = 11
STATES = 2048
ZZ_RATE = 0.06
F32 = jnp.float32
BF16 = jnp.bfloat16

SIZES = [math.comb(GS, k) for k in range(GS + 1)]
PROP_ROWS = 5512
GROUPS = [
    (0, 232, 0, 256, 0, 240),
    (232, 330, 256, 384, 240, 336),
    (562, 462, 640, 512, 576, 464),
    (1024, 462, 1152, 512, 1040, 464),
    (1486, 330, 1664, 384, 1504, 336),
    (1816, 232, 2048, 256, 1840, 240),
]
U_ROWS = 2304
B_ROWS = 2080
UNROLL = 16


def lay_out_blocks(flat, blocks):
    starts = []
    at = 0
    for n in SIZES:
        starts.append(at)
        at += n * n
    lane = lax.broadcasted_iota(jnp.int32, (8, 128), 1)

    def shifted(piece_of, count, shift, columns):
        pieces = []
        for i in range(columns + (1 if shift else 0)):
            piece = piece_of(i)
            pieces.append(pltpu.roll(piece, 128 - shift, 1) if shift else piece)
        if not shift:
            return pieces
        keep = lane[:count] < 128 - shift
        return [jnp.where(keep, pieces[i], pieces[i + 1]) for i in range(columns)]

    for degree, group in ((4, 1), (5, 2), (6, 3), (7, 4)):
        n = SIZES[degree]
        row0 = GROUPS[group][4]
        columns = -(-n // 128)
        step = n // 2
        for s in range(64):
            count = len(range(s, n, 64))
            first, shift = divmod(starts[degree] + n * s, 128)
            rows = shifted(
                lambda i: flat[pl.ds(first + i, count, stride=step), :], count, shift, columns
            )
            for i in range(columns):
                blocks[pl.ds(i * B_ROWS + row0 + s, count, stride=64), :] = rows[i]
    for group, degrees in ((0, (0, 1, 2, 3)), (5, (8, 9, 10, 11))):
        row0 = GROUPS[group][4]
        column = 0
        for degree in degrees:
            n = SIZES[degree]
            for r in range(n):
                origin = starts[degree] + n * r - column
                first, shift = divmod(origin, 128)
                for i in range(2):
                    low, high = max(column, 128 * i), min(column + n, 128 * i + 128)
                    if low >= high:
                        blocks[pl.ds(i * B_ROWS + row0 + column + r, 1), :] = jnp.zeros((1, 128), F32)
                        continue
                    low, high = low - 128 * i, high - 128 * i
                    value = None
                    if low < 128 - shift:
                        value = flat[pl.ds(first + i, 1), :]
                        if shift:
                            value = pltpu.roll(value, 128 - shift, 1)
                    if shift and high > 128 - shift:
                        after = pltpu.roll(flat[pl.ds(first + i + 1, 1), :], 128 - shift, 1)
                        value = (
                            after
                            if value is None
                            else jnp.where(lane[:1] < 128 - shift, value, after)
                        )
                    if low > 0 or high < 128:
                        value = jnp.where((lane[:1] >= low) & (lane[:1] < high), value, 0.0)
                    blocks[pl.ds(i * B_ROWS + row0 + column + r, 1), :] = value
            column += n


def split_blocks(blocks, hi, lo):
    def body(t, carry):
        at = pl.multiple_of(t * 16, 16)
        rows = pl.ds(at, 16)
        for i in range(4):
            x = blocks[pl.ds(i * B_ROWS + at, 16), :]
            h = x.astype(BF16)
            hi[rows, i * 128 : (i + 1) * 128] = h
            lo[rows, i * 128 : (i + 1) * 128] = (x - h.astype(F32)).astype(BF16)
        return carry

    lax.fori_loop(0, B_ROWS // 16, body, 0)


def clear_pads(u):
    for _, n, at, rows, _, _ in GROUPS:
        u[pl.ds(at + n, rows - n), :] = jnp.zeros((rows - n, 128), F32)


def over_rows(move):
    for number, (first, n, _, _, _, _) in enumerate(GROUPS):

        def body(t, carry):
            base = pl.multiple_of(t * UNROLL, UNROLL)
            for i in range(UNROLL):
                move(number, first + base + i, base + i)
            return carry

        whole = n // UNROLL
        lax.fori_loop(0, whole, body, 0)
        for r in range(whole * UNROLL, n):
            move(number, first + r, r)


def gather(source, u, table, offset):
    def move(number, j, r):
        u[pl.ds(GROUPS[number][2] + r, 1), :] = source[pl.ds(table[offset + j], 1), :]

    over_rows(move)


def scatter(y, target, table, offset):
    def move(number, j, r):
        target[pl.ds(table[offset + j], 1), :] = y[pl.ds(GROUPS[number][4] + r, 1), :]

    over_rows(move)


def scatter_lanes(y, target, table, offset):
    group_of_lane = lax.shift_right_logical(lax.broadcasted_iota(jnp.int32, (1, 128), 1), 5)

    def move(number, j, r):
        code = table[offset + j]
        row = lax.shift_right_logical(code, 2)
        pltpu.store(
            target.at[pl.ds(row, 1), :],
            y[pl.ds(GROUPS[number][4] + r, 1), :],
            mask=group_of_lane == (code & 3),
        )

    over_rows(move)


def multiply(u, y, hi, lo):
    for _, _, u_at, k, b_at, m in GROUPS:
        x = u[pl.ds(u_at, k), :]
        xh = x.astype(BF16)
        xl = (x - xh.astype(F32)).astype(BF16)
        h = hi[pl.ds(b_at, m), :k]
        both = jnp.dot(h, jnp.concatenate([xh, xl], axis=1), preferred_element_type=F32)
        rest = jnp.dot(lo[pl.ds(b_at, m), :k], xh, preferred_element_type=F32)
        y[pl.ds(b_at, m), :] = both[:, :128] + both[:, 128:] + rest


def spread(value, source, at):
    rows = value.shape[0]
    group_of_lane = lax.shift_right_logical(lax.broadcasted_iota(jnp.int32, (rows, 128), 1), 5)
    turned = [value] + [pltpu.roll(value, 32 * t, 1) for t in (1, 2, 3)]
    for g in range(4):
        out = turned[(0 - g) % 4]
        for t in (1, 2, 3):
            out = jnp.where(group_of_lane == t, turned[(t - g) % 4], out)
        source[pl.ds(512 * g + at, rows), :] = out


def spread_all(values, source):
    def body(t, carry):
        at = pl.multiple_of(t * 32, 32)
        spread(values(at, 32), source, at)
        return carry

    lax.fori_loop(0, 16, body, 0)


def turn_in(block, source, g):
    source[pl.ds(128 * g, 128), :] = jnp.concatenate([block] * 4, axis=0).T


def turn_all(folded, source):
    for g in range(16):
        turn_in(folded[pl.ds(32 * g, 32), :], source, g)


def turn_out(source, out):
    for g in range(16):
        out[pl.ds(g, 32, stride=16), :] = source[pl.ds(128 * g, 128), :].T[:32]


def spin(index, position):
    return 1 - 2 * (lax.shift_right_logical(index, position) & 1)


def first_kernel(table, levels, wave, flat, out, hi, lo, blocks, u, y, source, folded):
    device = lax.axis_index("wide") * 8 + lax.axis_index("narrow")
    high = jnp.int32(0)
    for s in range(8):
        high = high + levels[LB + s] * spin(device, s) * spin(device, s + 1)
    border = levels[LB - 1] * spin(device, 0)
    lane = lax.broadcasted_iota(jnp.int32, (32, 128), 1)
    lane_energy = jnp.zeros((32, 128), jnp.int32) + high
    for s in range(6):
        lane_energy = lane_energy + levels[s] * (spin(lane, s) * spin(lane, s + 1))
    last_lane_spin = spin(lane, 6)

    def phased(at, rows):
        row = lax.broadcasted_iota(jnp.int32, (32, 128), 0) + at
        spins = [spin(row, s) for s in range(9)]
        energy = lane_energy + levels[6] * (last_lane_spin * spins[0]) + border * spins[8]
        for s in range(8):
            energy = energy + levels[7 + s] * (spins[s] * spins[s + 1])
        return wave[pl.ds(at, rows), :] * jnp.exp(-ZZ_RATE * energy.astype(F32))

    lay_out_blocks(flat, blocks)
    split_blocks(blocks, hi, lo)
    clear_pads(u)
    spread_all(phased, source)
    gather(source, u, table, 0)
    multiply(u, y, hi, lo)
    scatter_lanes(y, folded, table, STATES)
    turn_all(folded, source)
    gather(source, u, table, 2 * STATES)
    multiply(u, y, hi, lo)
    scatter(y, source, table, 3 * STATES)
    turn_out(source, out)


def second_kernel(table, amplitudes, hi, lo, out, u, y, source):
    clear_pads(u)
    spread_all(lambda at, rows: amplitudes[pl.ds(at, rows), :], source)
    gather(source, u, table, 0)
    multiply(u, y, hi, lo)
    scatter_lanes(y, out, table, STATES)


def third_kernel(table, amplitudes, hi, lo, out, u, y, source, folded):
    clear_pads(u)
    for g in range(16):
        turn_in(amplitudes[pl.ds(g, 32, stride=16), :], source, g)
    gather(source, u, table, 0)
    multiply(u, y, hi, lo)
    scatter_lanes(y, folded, table, STATES)
    turn_all(folded, source)
    gather(source, u, table, 2 * STATES)
    multiply(u, y, hi, lo)
    scatter_lanes(y, folded, table, 3 * STATES)
    turn_all(folded, source)
    gather(source, u, table, 4 * STATES)
    multiply(u, y, hi, lo)
    scatter(y, source, table, 5 * STATES)
    turn_out(source, out)


SMEM = pl.BlockSpec(memory_space=pltpu.SMEM)
VMEM = pl.BlockSpec(memory_space=pltpu.VMEM)
AMPLITUDES = jax.ShapeDtypeStruct((512, 128), F32)
BLOCKS = jax.ShapeDtypeStruct((B_ROWS, 512), BF16)
U = pltpu.VMEM((U_ROWS, 128), F32)
Y = pltpu.VMEM((B_ROWS, 128), F32)
SOURCE = pltpu.VMEM((STATES, 128), F32)
FOLDED = pltpu.VMEM((512, 128), F32)


def index_tables(gate_orders, sector_order):
    mapped = jnp.zeros((gate_orders.shape[0], STATES), jnp.int32)
    for position in range(GS):
        chosen = jnp.right_shift(sector_order, position) & 1
        mapped = mapped + jnp.left_shift(chosen[None, :], gate_orders[:, position : position + 1])
    c0, c1, c2, c3, c4, c5 = (mapped[g] for g in range(6))

    def quarters(c):
        return (c & 3) * 512 + (c >> 2)

    def fold_top(c):
        mid = c & 63
        return ((mid >> 2) * 32 + (c >> 6)) * 4 + (mid & 3)

    def fold_low(c):
        mid = c >> 5
        return ((mid >> 2) * 32 + (c & 31)) * 4 + (mid & 3)

    first = jnp.concatenate([quarters(c0), fold_top(c0), c1, c1])
    second = jnp.concatenate([quarters(c2), c2])
    third = jnp.concatenate(
        [c3, fold_low(c3), (c4 & 63) * 32 + (c4 >> 6), fold_top(c4), c5, c5]
    )
    return first, second, third


def exchange(amplitudes):
    return lax.all_to_all(amplitudes, ("narrow", "wide"), split_axis=0, concat_axis=0, tiled=True)


def shards(wavefunction, propagator, gate_orders, sector_order, bond_level):
    first, second, third = index_tables(gate_orders, sector_order)
    flat = jnp.pad(propagator, (0, PROP_ROWS * 128 - propagator.shape[0])).reshape(-1, 128)
    amplitudes, hi, lo = pl.pallas_call(
        first_kernel,
        out_shape=(AMPLITUDES, BLOCKS, BLOCKS),
        in_specs=[SMEM, SMEM, VMEM, VMEM],
        out_specs=(VMEM, VMEM, VMEM),
        scratch_shapes=[pltpu.VMEM((4 * B_ROWS, 128), F32), U, Y, SOURCE, FOLDED],
        name="first",
    )(first, bond_level, wavefunction.reshape(512, 128), flat)
    amplitudes = exchange(amplitudes)
    amplitudes = pl.pallas_call(
        second_kernel,
        out_shape=AMPLITUDES,
        in_specs=[SMEM, VMEM, VMEM, VMEM],
        out_specs=VMEM,
        scratch_shapes=[U, Y, SOURCE],
        name="second",
    )(second, amplitudes, hi, lo)
    amplitudes = exchange(amplitudes)
    amplitudes = pl.pallas_call(
        third_kernel,
        out_shape=AMPLITUDES,
        in_specs=[SMEM, VMEM, VMEM, VMEM],
        out_specs=VMEM,
        scratch_shapes=[U, Y, SOURCE, FOLDED],
        name="third",
    )(third, amplitudes, hi, lo)
    return amplitudes.reshape(-1)


def solution(mesh):
    in_specs = (P(("wide", "narrow")), P(), P(), P(), P())
    out_specs = P(("wide", "narrow"))
    return jax.shard_map(shards, mesh=mesh, in_specs=in_specs, out_specs=out_specs, check_vma=False)
```

```python
import math

import jax
import jax.numpy as jnp
from jax import lax
from jax.experimental import pallas as pl
from jax.experimental.pallas import tpu as pltpu
from jax.sharding import PartitionSpec as P

LB = 16
GS = 11
STATES = 2048
ZZ_RATE = 0.06
F32 = jnp.float32
BF16 = jnp.bfloat16

SIZES = [math.comb(GS, k) for k in range(GS + 1)]
PROP_ROWS = 5512
NT = (((1,), (1,)), ((), ()))
GROUPS = [
    (0, 232, 0, 256),
    (232, 330, 256, 384),
    (562, 462, 640, 512),
    (1024, 462, 1152, 512),
    (1486, 330, 1664, 384),
    (1816, 232, 2048, 256),
]
PADDED = 2304
PADDED_BLOCKS = PADDED // 128
BLOCKS = STATES // 128


def lay_out_blocks(flat, blocks):
    starts = []
    at = 0
    for n in SIZES:
        starts.append(at)
        at += n * n
    lane = lax.broadcasted_iota(jnp.int32, (8, 128), 1)

    def shifted(piece_of, count, shift, columns):
        pieces = []
        for i in range(columns + (1 if shift else 0)):
            piece = piece_of(i)
            pieces.append(pltpu.roll(piece, 128 - shift, 1) if shift else piece)
        if not shift:
            return pieces
        keep = lane[:count] < 128 - shift
        return [jnp.where(keep, pieces[i], pieces[i + 1]) for i in range(columns)]

    for degree, group in ((4, 1), (5, 2), (6, 3), (7, 4)):
        n = SIZES[degree]
        row0 = GROUPS[group][2]
        columns = -(-n // 128)
        step = n // 2
        for s in range(64):
            count = len(range(s, n, 64))
            first, shift = divmod(starts[degree] + n * s, 128)
            rows = shifted(
                lambda i: flat[pl.ds(first + i, count, stride=step), :], count, shift, columns
            )
            for i in range(columns):
                blocks[pl.ds(i * PADDED + row0 + s, count, stride=64), :] = rows[i]
    for group, degrees in ((0, (0, 1, 2, 3)), (5, (8, 9, 10, 11))):
        row0 = GROUPS[group][2]
        column = 0
        for degree in degrees:
            n = SIZES[degree]
            for r in range(n):
                origin = starts[degree] + n * r - column
                first, shift = divmod(origin, 128)
                for i in range(2):
                    low, high = max(column, 128 * i), min(column + n, 128 * i + 128)
                    if low >= high:
                        blocks[pl.ds(i * PADDED + row0 + column + r, 1), :] = jnp.zeros((1, 128), F32)
                        continue
                    low, high = low - 128 * i, high - 128 * i
                    value = None
                    if low < 128 - shift:
                        value = flat[pl.ds(first + i, 1), :]
                        if shift:
                            value = pltpu.roll(value, 128 - shift, 1)
                    if shift and high > 128 - shift:
                        after = pltpu.roll(flat[pl.ds(first + i + 1, 1), :], 128 - shift, 1)
                        value = (
                            after
                            if value is None
                            else jnp.where(lane[:1] < 128 - shift, value, after)
                        )
                    if low > 0 or high < 128:
                        value = jnp.where((lane[:1] >= low) & (lane[:1] < high), value, 0.0)
                    blocks[pl.ds(i * PADDED + row0 + column + r, 1), :] = value
            column += n


def split_blocks(blocks, hi, lo):
    def body(t, carry):
        at = pl.multiple_of(t * 16, 16)
        rows = pl.ds(at, 16)
        for i in range(4):
            x = blocks[pl.ds(i * PADDED + at, 16), :]
            h = x.astype(BF16)
            hi[rows, i * 128 : (i + 1) * 128] = h
            lo[rows, i * 128 : (i + 1) * 128] = (x - h.astype(F32)).astype(BF16)
        return carry

    lax.fori_loop(0, PADDED // 16, body, 0)


def pad_order(order, padded):
    lane = lax.broadcasted_iota(jnp.int32, (1, 128), 1)
    for first, n, at, rows in GROUPS:
        for r in range(0, rows, 128):
            block, shift = divmod(first + r, 128)
            value = order[pl.ds(min(block, BLOCKS - 1), 1), :]
            if shift:
                after = order[pl.ds(min(block + 1, BLOCKS - 1), 1), :]
                value = jnp.where(
                    lane < 128 - shift,
                    pltpu.roll(value, 128 - shift, 1),
                    pltpu.roll(after, 128 - shift, 1),
                )
            if r + 128 > n:
                value = jnp.where(lane < n - r, value, -1)
            padded[pl.ds((at + r) // 128, 1), :] = value
    spare = 24 - PADDED_BLOCKS
    padded[pl.ds(PADDED_BLOCKS, spare), :] = jnp.full((spare, 128), -1, jnp.int32)


def invert_order(padded, places):
    total = jnp.zeros((32, 128), F32)
    lane = lax.broadcasted_iota(jnp.int32, (16, 128), 1)
    row = lax.broadcasted_iota(jnp.int32, (16, 128), 0)
    column = lax.broadcasted_iota(jnp.int32, (128, 128), 0)
    for o in range(PADDED_BLOCKS):
        state = padded[pl.ds(o, 1), :]
        place = lane + 128 * o
        hit = lax.shift_right_arithmetic(state, 7) == row
        left = jnp.concatenate(
            [
                jnp.where(hit, lax.shift_right_logical(place, 4).astype(F32), 0.0),
                jnp.where(hit, (place & 15).astype(F32), 0.0),
            ],
            axis=0,
        ).astype(BF16)
        right = jnp.where((state & 127) == column, 1.0, 0.0).astype(BF16)
        total = total + lax.dot_general(left, right, NT, preferred_element_type=F32)
    places[...] = (16.0 * total[:16] + total[16:]).astype(jnp.int32)


def take(row, index):
    return jnp.take_along_axis(row, index, axis=1, mode="promise_in_bounds")


def tables(orders, gate, top, padded, places, pull, push):
    state = padded[...]
    mapped = jnp.zeros_like(state)
    for t in range(GS):
        mapped = mapped + lax.shift_left(
            lax.shift_right_logical(state, t) & 1, jnp.full_like(state, orders[gate, t])
        )
    if top:
        mapped = (mapped & 3) * 512 + lax.shift_right_logical(mapped, 2)
    pull[...] = jnp.where(state < 0, -1, mapped)
    for half in range(2):
        place = lax.broadcasted_iota(jnp.int32, (8, 128), 0) * 128 + lax.broadcasted_iota(
            jnp.int32, (8, 128), 1
        )
        place = place + half * 1024
        if top:
            place = (place & 511) * 4 + lax.shift_right_logical(place, 9)
        state = jnp.zeros_like(place)
        for t in range(GS):
            bit = lax.shift_right_logical(place, jnp.full_like(place, orders[gate, t])) & 1
            state = state + bit * (1 << t)
        block, lane = lax.shift_right_logical(state, 7), state & 127
        found = jnp.zeros_like(place)
        for i in range(BLOCKS):
            row = jnp.broadcast_to(places[pl.ds(i, 1), :], (8, 128))
            found = jnp.where(block == i, take(row, lane), found)
        push[pl.ds(8 * half, 8), :] = found


def permute(source, target, table, source_blocks, target_blocks, unroll):
    def body(t, carry):
        for step in range(unroll):
            o = t * unroll + step
            index = jnp.broadcast_to(table[pl.ds(o, 1), :], (8, 128))
            block, lane = lax.shift_right_arithmetic(index, 7), index & 127
            hits = [block == i for i in range(source_blocks)]
            for b in range(4):
                found = jnp.zeros((8, 128), F32)
                for i in range(source_blocks):
                    piece = source[8 * b : 8 * b + 8, 128 * i : 128 * i + 128]
                    found = jnp.where(hits[i], take(piece, lane), found)
                target[8 * b : 8 * b + 8, pl.ds(pl.multiple_of(o * 128, 128), 128)] = found
        return carry

    lax.fori_loop(0, target_blocks // unroll, body, 0)


def multiply(u, y, hi, lo):
    for _, _, at, k in GROUPS:
        x = u[:, at : at + k]
        xh = x.astype(BF16)
        xl = (x - xh.astype(F32)).astype(BF16)
        both = lax.dot_general(
            jnp.concatenate([xh, xl], axis=0),
            hi[at : at + k, :k],
            NT,
            preferred_element_type=F32,
        )
        rest = lax.dot_general(xh, lo[at : at + k, :k], NT, preferred_element_type=F32)
        y[:, at : at + k] = both[:32] + both[32:] + rest


def gate(orders, number, top, x, u, y, hi, lo, padded, places, pull, push):
    tables(orders, number, top, padded, places, pull, push)
    permute(x, u, pull, BLOCKS, PADDED_BLOCKS, 3)
    multiply(u, y, hi, lo)
    permute(y, x, push, PADDED_BLOCKS, BLOCKS, 2)


def turn_in(value, at, x):
    turned = value.T
    for g in range(4):
        x[:, 512 * g + at : 512 * g + at + 128] = turned[32 * g : 32 * g + 32]


def top_in(amplitudes, x):
    for at in range(0, 512, 128):
        turn_in(amplitudes[pl.ds(at, 128), :], at, x)


def top_out(x, out):
    for at in range(0, 512, 128):
        pieces = [x[:, 512 * g + at : 512 * g + at + 128] for g in range(4)]
        out[pl.ds(at, 128), :] = jnp.concatenate(pieces, axis=0).T


def low_in(amplitudes, x):
    for g in range(16):
        x[:, 128 * g : 128 * g + 128] = amplitudes[pl.ds(g, 32, stride=16), :]


def low_out(x, out):
    for g in range(16):
        out[pl.ds(g, 32, stride=16), :] = x[:, 128 * g : 128 * g + 128]


def spin(index, position):
    return 1 - 2 * (lax.shift_right_logical(index, position) & 1)


def first_kernel(
    orders, levels, order, wave, flat, out, hi, lo, padded, places, blocks, x, u, y, pull, push, plain
):
    device = lax.axis_index("wide") * 8 + lax.axis_index("narrow")
    high = jnp.int32(0)
    for s in range(8):
        high = high + levels[LB + s] * spin(device, s) * spin(device, s + 1)
    border = levels[LB - 1] * spin(device, 0)
    lane = lax.broadcasted_iota(jnp.int32, (128, 128), 1)
    lane_energy = jnp.zeros((128, 128), jnp.int32) + high
    for s in range(6):
        lane_energy = lane_energy + levels[s] * (spin(lane, s) * spin(lane, s + 1))
    last_lane_spin = spin(lane, 6)

    lay_out_blocks(flat, blocks)
    split_blocks(blocks, hi, lo)
    pad_order(order, padded)
    invert_order(padded, places)
    for at in range(0, 512, 128):
        row = lax.broadcasted_iota(jnp.int32, (128, 128), 0) + at
        spins = [spin(row, s) for s in range(9)]
        energy = lane_energy + levels[6] * (last_lane_spin * spins[0]) + border * spins[8]
        for s in range(8):
            energy = energy + levels[7 + s] * (spins[s] * spins[s + 1])
        turn_in(wave[pl.ds(at, 128), :] * jnp.exp(-ZZ_RATE * energy.astype(F32)), at, x)
    rest = (x, u, y, hi, lo, padded, places, pull, push)
    gate(orders, 0, True, *rest)
    top_out(x, plain)
    low_in(plain, x)
    gate(orders, 1, False, *rest)
    low_out(x, out)


def second_kernel(orders, amplitudes, hi, lo, padded, places, out, x, u, y, pull, push):
    top_in(amplitudes, x)
    gate(orders, 2, True, x, u, y, hi, lo, padded, places, pull, push)
    top_out(x, out)


def third_kernel(orders, amplitudes, hi, lo, padded, places, out, x, u, y, pull, push, plain):
    rest = (x, u, y, hi, lo, padded, places, pull, push)
    low_in(amplitudes, x)
    gate(orders, 3, False, *rest)
    low_out(x, plain)
    top_in(plain, x)
    gate(orders, 4, True, *rest)
    top_out(x, plain)
    low_in(plain, x)
    gate(orders, 5, False, *rest)
    low_out(x, out)


SMEM = pl.BlockSpec(memory_space=pltpu.SMEM)
VMEM = pl.BlockSpec(memory_space=pltpu.VMEM)
AMPLITUDES = jax.ShapeDtypeStruct((512, 128), F32)
HALVES = jax.ShapeDtypeStruct((PADDED, 512), BF16)
SCRATCH = [
    pltpu.VMEM((32, STATES), F32),
    pltpu.VMEM((32, PADDED), F32),
    pltpu.VMEM((32, PADDED), F32),
    pltpu.VMEM((24, 128), jnp.int32),
    pltpu.VMEM((16, 128), jnp.int32),
]
PLAIN = pltpu.VMEM((512, 128), F32)


def exchange(amplitudes):
    return lax.all_to_all(amplitudes, ("narrow", "wide"), split_axis=0, concat_axis=0, tiled=True)


def shards(wavefunction, propagator, gate_orders, sector_order, bond_level):
    flat = jnp.pad(propagator, (0, PROP_ROWS * 128 - propagator.shape[0])).reshape(-1, 128)
    amplitudes, *rest = pl.pallas_call(
        first_kernel,
        out_shape=(
            AMPLITUDES,
            HALVES,
            HALVES,
            jax.ShapeDtypeStruct((24, 128), jnp.int32),
            jax.ShapeDtypeStruct((16, 128), jnp.int32),
        ),
        in_specs=[SMEM, SMEM, VMEM, VMEM, VMEM],
        out_specs=(VMEM,) * 5,
        scratch_shapes=[pltpu.VMEM((4 * PADDED, 128), F32), *SCRATCH, PLAIN],
        name="first",
    )(gate_orders, bond_level, sector_order.reshape(16, 128), wavefunction.reshape(512, 128), flat)
    amplitudes = exchange(amplitudes)
    amplitudes = pl.pallas_call(
        second_kernel,
        out_shape=AMPLITUDES,
        in_specs=[SMEM] + [VMEM] * 5,
        out_specs=VMEM,
        scratch_shapes=SCRATCH,
        name="second",
    )(gate_orders, amplitudes, *rest)
    amplitudes = exchange(amplitudes)
    amplitudes = pl.pallas_call(
        third_kernel,
        out_shape=AMPLITUDES,
        in_specs=[SMEM] + [VMEM] * 5,
        out_specs=VMEM,
        scratch_shapes=[*SCRATCH, PLAIN],
        name="third",
    )(gate_orders, amplitudes, *rest)
    return amplitudes.reshape(-1)


def solution(mesh):
    in_specs = (P(("wide", "narrow")), P(), P(), P(), P())
    out_specs = P(("wide", "narrow"))
    return jax.shard_map(shards, mesh=mesh, in_specs=in_specs, out_specs=out_specs, check_vma=False)
```

```python
import math

import jax
import jax.numpy as jnp
from jax import lax
from jax.experimental import pallas as pl
from jax.experimental.pallas import tpu as pltpu
from jax.sharding import PartitionSpec as P

LB = 16
GS = 11
STATES = 2048
ZZ_RATE = 0.06
F32 = jnp.float32
BF16 = jnp.bfloat16

SIZES = [math.comb(GS, k) for k in range(GS + 1)]
PROP_ROWS = 5512
NT = (((1,), (1,)), ((), ()))
GROUPS = [
    (0, 232, 0, 256),
    (232, 330, 256, 384),
    (562, 462, 640, 512),
    (1024, 462, 1152, 512),
    (1486, 330, 1664, 384),
    (1816, 232, 2048, 256),
]
PADDED = 2304
PADDED_BLOCKS = PADDED // 128
BLOCKS = STATES // 128


def lay_out_blocks(flat, blocks):
    starts = []
    at = 0
    for n in SIZES:
        starts.append(at)
        at += n * n
    lane = lax.broadcasted_iota(jnp.int32, (8, 128), 1)

    def shifted(piece_of, count, shift, columns):
        pieces = []
        for i in range(columns + (1 if shift else 0)):
            piece = piece_of(i)
            pieces.append(pltpu.roll(piece, 128 - shift, 1) if shift else piece)
        if not shift:
            return pieces
        keep = lane[:count] < 128 - shift
        return [jnp.where(keep, pieces[i], pieces[i + 1]) for i in range(columns)]

    for degree, group in ((4, 1), (5, 2), (6, 3), (7, 4)):
        n = SIZES[degree]
        row0 = GROUPS[group][2]
        columns = -(-n // 128)
        step = n // 2
        for s in range(64):
            count = len(range(s, n, 64))
            first, shift = divmod(starts[degree] + n * s, 128)
            rows = shifted(
                lambda i: flat[pl.ds(first + i, count, stride=step), :], count, shift, columns
            )
            for i in range(columns):
                blocks[pl.ds(i * PADDED + row0 + s, count, stride=64), :] = rows[i]
    for group, degrees in ((0, (0, 1, 2, 3)), (5, (8, 9, 10, 11))):
        row0 = GROUPS[group][2]
        column = 0
        for degree in degrees:
            small_sector(flat, blocks, starts[degree], SIZES[degree], row0, column)
            column += SIZES[degree]


def small_sector(flat, blocks, start, n, row0, column):
    lane = lax.broadcasted_iota(jnp.int32, (8, 128), 1)
    row = lax.broadcasted_iota(jnp.int32, (8, 128), 0)
    step, extra = divmod(n, 128)
    sides = [i for i in range(2) if max(column, 128 * i) < min(column + n, 128 * i + 128)]
    for r in range(0, n, 8):
        count = min(8, n - r)
        first, shift = divmod(start + n * r - column, 128)
        spot = lane + (row * extra + shift)
        from_lane = spot & 127
        spot = lax.shift_right_logical(spot, 7)
        last = (shift + extra * (count - 1) + 127) >> 7
        turned = {}
        for m in range(min(sides), max(sides) + last + 1):
            if step:
                at = min(first + m, PROP_ROWS - 8)
                piece = flat[pl.ds(at, 8), :]
            else:
                at = min(first + m, PROP_ROWS - 1)
                piece = jnp.broadcast_to(flat[pl.ds(at, 1), :], (8, 128))
            turned[m] = take(piece, from_lane)
        for i in range(2):
            target = pl.ds(i * PADDED + row0 + column + r, count)
            if i not in sides:
                blocks[target, :] = jnp.zeros((count, 128), F32)
                continue
            value = turned[i]
            for m in range(1, last + 1):
                value = jnp.where(spot == m, turned[i + m], value)
            low, high = column - 128 * i, column + n - 128 * i
            if low > 0 or high < 128:
                value = jnp.where((lane >= low) & (lane < high), value, 0.0)
            blocks[target, :] = value[:count]


def split_blocks(blocks, hi, lo):
    def body(t, carry):
        at = pl.multiple_of(t * 16, 16)
        rows = pl.ds(at, 16)
        for i in range(4):
            x = blocks[pl.ds(i * PADDED + at, 16), :]
            h = x.astype(BF16)
            hi[rows, i * 128 : (i + 1) * 128] = h
            lo[rows, i * 128 : (i + 1) * 128] = (x - h.astype(F32)).astype(BF16)
        return carry

    lax.fori_loop(0, PADDED // 16, body, 0)


def pad_order(order, padded):
    lane = lax.broadcasted_iota(jnp.int32, (1, 128), 1)
    for first, n, at, rows in GROUPS:
        for r in range(0, rows, 128):
            block, shift = divmod(first + r, 128)
            value = order[pl.ds(min(block, BLOCKS - 1), 1), :]
            if shift:
                after = order[pl.ds(min(block + 1, BLOCKS - 1), 1), :]
                value = jnp.where(
                    lane < 128 - shift,
                    pltpu.roll(value, 128 - shift, 1),
                    pltpu.roll(after, 128 - shift, 1),
                )
            if r + 128 > n:
                value = jnp.where(lane < n - r, value, -1)
            padded[pl.ds((at + r) // 128, 1), :] = value
    spare = 24 - PADDED_BLOCKS
    padded[pl.ds(PADDED_BLOCKS, spare), :] = jnp.full((spare, 128), -1, jnp.int32)


def invert_order(padded, places):
    total = jnp.zeros((32, 128), F32)
    lane = lax.broadcasted_iota(jnp.int32, (16, 128), 1)
    row = lax.broadcasted_iota(jnp.int32, (16, 128), 0)
    column = lax.broadcasted_iota(jnp.int32, (128, 128), 0)
    for o in range(PADDED_BLOCKS):
        state = padded[pl.ds(o, 1), :]
        place = lane + 128 * o
        hit = lax.shift_right_arithmetic(state, 7) == row
        left = jnp.concatenate(
            [
                jnp.where(hit, lax.shift_right_logical(place, 4).astype(F32), 0.0),
                jnp.where(hit, (place & 15).astype(F32), 0.0),
            ],
            axis=0,
        ).astype(BF16)
        right = jnp.where((state & 127) == column, 1.0, 0.0).astype(BF16)
        total = total + lax.dot_general(left, right, NT, preferred_element_type=F32)
    places[...] = (16.0 * total[:16] + total[16:]).astype(jnp.int32)


def take(row, index):
    return jnp.take_along_axis(row, index, axis=1, mode="promise_in_bounds")


def tables(orders, gate, top, padded, places, pull, push):
    state = padded[...]
    mapped = jnp.zeros_like(state)
    for t in range(GS):
        mapped = mapped + lax.shift_left(
            lax.shift_right_logical(state, t) & 1, jnp.full_like(state, orders[gate, t])
        )
    if top:
        mapped = (mapped & 3) * 512 + lax.shift_right_logical(mapped, 2)
    pull[...] = jnp.where(state < 0, -1, mapped)
    for half in range(2):
        place = lax.broadcasted_iota(jnp.int32, (8, 128), 0) * 128 + lax.broadcasted_iota(
            jnp.int32, (8, 128), 1
        )
        place = place + half * 1024
        if top:
            place = (place & 511) * 4 + lax.shift_right_logical(place, 9)
        state = jnp.zeros_like(place)
        for t in range(GS):
            bit = lax.shift_right_logical(place, jnp.full_like(place, orders[gate, t])) & 1
            state = state + bit * (1 << t)
        block, lane = lax.shift_right_logical(state, 7), state & 127
        found = jnp.zeros_like(place)
        for i in range(BLOCKS):
            row = jnp.broadcast_to(places[pl.ds(i, 1), :], (8, 128))
            found = jnp.where(block == i, take(row, lane), found)
        push[pl.ds(8 * half, 8), :] = found


def move_block(source, target, table, source_blocks, o):
    index = jnp.broadcast_to(table[pl.ds(o, 1), :], (8, 128))
    block, lane = lax.shift_right_arithmetic(index, 7), index & 127
    hits = [block == i for i in range(source_blocks)]
    for b in range(4):
        found = jnp.zeros((8, 128), F32)
        for i in range(source_blocks):
            piece = source[8 * b : 8 * b + 8, 128 * i : 128 * i + 128]
            found = jnp.where(hits[i], take(piece, lane), found)
        at = o * 128 if isinstance(o, int) else pl.multiple_of(o * 128, 128)
        target[8 * b : 8 * b + 8, pl.ds(at, 128)] = found


def multiply(u, y, hi, lo, at, k):
    x = u[:, at : at + k]
    xh = x.astype(BF16)
    xl = (x - xh.astype(F32)).astype(BF16)
    both = lax.dot_general(
        jnp.concatenate([xh, xl], axis=0), hi[at : at + k, :k], NT, preferred_element_type=F32
    )
    rest = lax.dot_general(xh, lo[at : at + k, :k], NT, preferred_element_type=F32)
    y[:, at : at + k] = both[:32] + both[32:] + rest


def gate(orders, number, top, x, u, y, hi, lo, padded, places, pull, push, ready=None):
    tables(orders, number, top, padded, places, pull, push)
    for group, (_, _, at, k) in enumerate(GROUPS):
        for o in range(at // 128, (at + k) // 128):
            move_block(x, u, pull, BLOCKS, o)
        if ready is not None:
            ready(group)
        multiply(u, y, hi, lo, at, k)
    scatter(x, y, push)


def scatter(x, y, push):
    def body(t, carry):
        for step in range(8):
            move_block(y, x, push, PADDED_BLOCKS, t * 8 + step)
        return carry

    lax.fori_loop(0, BLOCKS // 8, body, 0)


def half_copies(hi_from, lo_from, hi_to, lo_to, sems):
    copies = []
    for group, (_, _, at, k) in enumerate(GROUPS):
        rows = pl.ds(at, k)
        copies.append(
            (
                pltpu.make_async_copy(hi_from.at[rows, :], hi_to.at[rows, :], sems.at[2 * group]),
                pltpu.make_async_copy(lo_from.at[rows, :], lo_to.at[rows, :], sems.at[2 * group + 1]),
            )
        )
    return copies


def fetch(hi_hbm, lo_hbm, hi, lo, sems):
    copies = half_copies(hi_hbm, lo_hbm, hi, lo, sems)
    for pair in copies:
        for copy in pair:
            copy.start()

    def ready(group):
        for copy in copies[group]:
            copy.wait()

    return ready


def turn_in(value, at, x):
    turned = value.T
    for g in range(4):
        x[:, 512 * g + at : 512 * g + at + 128] = turned[32 * g : 32 * g + 32]


def top_in(amplitudes, x):
    for at in range(0, 512, 128):
        turn_in(amplitudes[pl.ds(at, 128), :], at, x)


def top_out(x, out):
    for at in range(0, 512, 128):
        pieces = [x[:, 512 * g + at : 512 * g + at + 128] for g in range(4)]
        out[pl.ds(at, 128), :] = jnp.concatenate(pieces, axis=0).T


def low_in(amplitudes, x):
    for g in range(16):
        x[:, 128 * g : 128 * g + 128] = amplitudes[pl.ds(g, 32, stride=16), :]


def low_out(x, out):
    for g in range(16):
        out[pl.ds(g, 32, stride=16), :] = x[:, 128 * g : 128 * g + 128]


def spin(index, position):
    return 1 - 2 * (lax.shift_right_logical(index, position) & 1)


def first_kernel(
    orders, levels, order, wave, tail, propagator,
    out, hi_hbm, lo_hbm, padded, places,
    flat, blocks, hi, lo, x, u, y, pull, push, plain, flat_sem, sems,
):
    length = (PROP_ROWS - 1) * 128
    load = pltpu.make_async_copy(
        propagator.at[pl.ds(0, length)],
        flat.reshape(PROP_ROWS * 128).at[pl.ds(0, length)],
        flat_sem,
    )
    load.start()
    device = lax.axis_index("wide") * 8 + lax.axis_index("narrow")
    high = jnp.int32(0)
    for s in range(8):
        high = high + levels[LB + s] * spin(device, s) * spin(device, s + 1)
    border = levels[LB - 1] * spin(device, 0)
    lane = lax.broadcasted_iota(jnp.int32, (128, 128), 1)
    lane_energy = jnp.zeros((128, 128), jnp.int32) + high
    for s in range(6):
        lane_energy = lane_energy + levels[s] * (spin(lane, s) * spin(lane, s + 1))
    last_lane_spin = spin(lane, 6)
    pad_order(order, padded)
    invert_order(padded, places)
    for at in range(0, 512, 128):
        row = lax.broadcasted_iota(jnp.int32, (128, 128), 0) + at
        spins = [spin(row, s) for s in range(9)]
        energy = lane_energy + levels[6] * (last_lane_spin * spins[0]) + border * spins[8]
        for s in range(8):
            energy = energy + levels[7 + s] * (spins[s] * spins[s + 1])
        turn_in(wave[pl.ds(at, 128), :] * jnp.exp(-ZZ_RATE * energy.astype(F32)), at, x)
    load.wait()
    flat[pl.ds(PROP_ROWS - 1, 1), :] = tail[...]
    lay_out_blocks(flat, blocks)
    split_blocks(blocks, hi, lo)
    saves = half_copies(hi, lo, hi_hbm, lo_hbm, sems)
    for pair in saves:
        for copy in pair:
            copy.start()
    rest = (x, u, y, hi, lo, padded, places, pull, push)
    gate(orders, 0, True, *rest)
    top_out(x, plain)
    low_in(plain, x)
    gate(orders, 1, False, *rest)
    low_out(x, out)
    for pair in saves:
        for copy in pair:
            copy.wait()


def second_kernel(
    orders, amplitudes, padded, places, hi_hbm, lo_hbm, out, hi, lo, x, u, y, pull, push, sems
):
    ready = fetch(hi_hbm, lo_hbm, hi, lo, sems)
    top_in(amplitudes, x)
    gate(orders, 2, True, x, u, y, hi, lo, padded, places, pull, push, ready)
    top_out(x, out)


def third_kernel(
    orders, amplitudes, padded, places, hi_hbm, lo_hbm, out, hi, lo, x, u, y, pull, push, plain, sems
):
    ready = fetch(hi_hbm, lo_hbm, hi, lo, sems)
    rest = (x, u, y, hi, lo, padded, places, pull, push)
    low_in(amplitudes, x)
    gate(orders, 3, False, *rest, ready)
    low_out(x, plain)
    top_in(plain, x)
    gate(orders, 4, True, *rest)
    top_out(x, plain)
    low_in(plain, x)
    gate(orders, 5, False, *rest)
    low_out(x, out)


SMEM = pl.BlockSpec(memory_space=pltpu.SMEM)
VMEM = pl.BlockSpec(memory_space=pltpu.VMEM)
ANY = pl.BlockSpec(memory_space=pl.ANY)
AMPLITUDES = jax.ShapeDtypeStruct((512, 128), F32)
HALVES = jax.ShapeDtypeStruct((PADDED, 512), BF16)
SCRATCH = [
    pltpu.VMEM((PADDED, 512), BF16),
    pltpu.VMEM((PADDED, 512), BF16),
    pltpu.VMEM((32, STATES), F32),
    pltpu.VMEM((32, PADDED), F32),
    pltpu.VMEM((32, PADDED), F32),
    pltpu.VMEM((24, 128), jnp.int32),
    pltpu.VMEM((16, 128), jnp.int32),
]
PLAIN = pltpu.VMEM((512, 128), F32)
SEMS = pltpu.SemaphoreType.DMA((12,))


def exchange(amplitudes):
    return lax.all_to_all(amplitudes, ("narrow", "wide"), split_axis=0, concat_axis=0, tiled=True)


def shards(wavefunction, propagator, gate_orders, sector_order, bond_level):
    length = (PROP_ROWS - 1) * 128
    tail = jnp.pad(propagator[length:], (0, PROP_ROWS * 128 - propagator.shape[0])).reshape(1, 128)
    amplitudes, hi, lo, padded, places = pl.pallas_call(
        first_kernel,
        out_shape=(
            AMPLITUDES,
            HALVES,
            HALVES,
            jax.ShapeDtypeStruct((24, 128), jnp.int32),
            jax.ShapeDtypeStruct((16, 128), jnp.int32),
        ),
        in_specs=[SMEM, SMEM, VMEM, VMEM, VMEM, ANY],
        out_specs=(VMEM, ANY, ANY, VMEM, VMEM),
        scratch_shapes=[
            pltpu.VMEM((PROP_ROWS, 128), F32),
            pltpu.VMEM((4 * PADDED, 128), F32),
            *SCRATCH,
            PLAIN,
            pltpu.SemaphoreType.DMA,
            SEMS,
        ],
        name="first",
    )(
        gate_orders,
        bond_level,
        sector_order.reshape(16, 128),
        wavefunction.reshape(512, 128),
        tail,
        propagator,
    )
    amplitudes = exchange(amplitudes)
    amplitudes = pl.pallas_call(
        second_kernel,
        out_shape=AMPLITUDES,
        in_specs=[SMEM, VMEM, VMEM, VMEM, ANY, ANY],
        out_specs=VMEM,
        scratch_shapes=[*SCRATCH, SEMS],
        name="second",
    )(gate_orders, amplitudes, padded, places, hi, lo)
    amplitudes = exchange(amplitudes)
    amplitudes = pl.pallas_call(
        third_kernel,
        out_shape=AMPLITUDES,
        in_specs=[SMEM, VMEM, VMEM, VMEM, ANY, ANY],
        out_specs=VMEM,
        scratch_shapes=[*SCRATCH, PLAIN, SEMS],
        name="third",
    )(gate_orders, amplitudes, padded, places, hi, lo)
    return amplitudes.reshape(-1)


def solution(mesh):
    in_specs = (P(("wide", "narrow")), P(), P(), P(), P())
    out_specs = P(("wide", "narrow"))
    return jax.shard_map(shards, mesh=mesh, in_specs=in_specs, out_specs=out_specs, check_vma=False)
```

```python
import math

import jax
import jax.numpy as jnp
from jax import lax
from jax.experimental import pallas as pl
from jax.experimental.pallas import tpu as pltpu
from jax.sharding import PartitionSpec as P

LB = 16
GS = 11
STATES = 2048
ZZ_RATE = 0.06
F32 = jnp.float32
BF16 = jnp.bfloat16

SIZES = [math.comb(GS, k) for k in range(GS + 1)]
PROP_ROWS = 5512
NT = (((1,), (1,)), ((), ()))
GROUPS = [
    (0, 232, 0, 256),
    (232, 330, 256, 384),
    (562, 462, 640, 512),
    (1024, 462, 1152, 512),
    (1486, 330, 1664, 384),
    (1816, 232, 2048, 256),
]
PADDED = 2304
PADDED_BLOCKS = PADDED // 128
BLOCKS = STATES // 128


def lay_out_blocks(flat, blocks):
    starts = []
    at = 0
    for n in SIZES:
        starts.append(at)
        at += n * n
    lane = lax.broadcasted_iota(jnp.int32, (8, 128), 1)

    def shifted(piece_of, count, shift, columns):
        pieces = []
        for i in range(columns + (1 if shift else 0)):
            piece = piece_of(i)
            pieces.append(pltpu.roll(piece, 128 - shift, 1) if shift else piece)
        if not shift:
            return pieces
        keep = lane[:count] < 128 - shift
        return [jnp.where(keep, pieces[i], pieces[i + 1]) for i in range(columns)]

    for degree, group in ((4, 1), (5, 2), (6, 3), (7, 4)):
        n = SIZES[degree]
        row0 = GROUPS[group][2]
        columns = -(-n // 128)
        step = n // 2
        placed = row0
        for s in range(64):
            count = len(range(s, n, 64))
            first, shift = divmod(starts[degree] + n * s, 128)
            rows = shifted(
                lambda i: flat[pl.ds(first + i, count, stride=step), :], count, shift, columns
            )
            for i in range(columns):
                blocks[pl.ds(i * PADDED + placed, count), :] = rows[i]
            placed += count
    for group, degrees in ((0, (0, 1, 2, 3)), (5, (8, 9, 10, 11))):
        row0 = GROUPS[group][2]
        column = 0
        for degree in degrees:
            small_sector(flat, blocks, starts[degree], SIZES[degree], row0, column)
            column += SIZES[degree]


def small_sector(flat, blocks, start, n, row0, column):
    lane = lax.broadcasted_iota(jnp.int32, (8, 128), 1)
    row = lax.broadcasted_iota(jnp.int32, (8, 128), 0)
    step, extra = divmod(n, 128)
    sides = [i for i in range(2) if max(column, 128 * i) < min(column + n, 128 * i + 128)]
    for r in range(0, n, 8):
        count = min(8, n - r)
        first, shift = divmod(start + n * r - column, 128)
        spot = lane + (row * extra + shift)
        from_lane = spot & 127
        spot = lax.shift_right_logical(spot, 7)
        last = (shift + extra * (count - 1) + 127) >> 7
        turned = {}
        for m in range(min(sides), max(sides) + last + 1):
            if step:
                at = min(first + m, PROP_ROWS - 8)
                piece = flat[pl.ds(at, 8), :]
            else:
                at = min(first + m, PROP_ROWS - 1)
                piece = jnp.broadcast_to(flat[pl.ds(at, 1), :], (8, 128))
            turned[m] = take(piece, from_lane)
        for i in range(2):
            target = pl.ds(i * PADDED + row0 + column + r, count)
            if i not in sides:
                blocks[target, :] = jnp.zeros((count, 128), F32)
                continue
            value = turned[i]
            for m in range(1, last + 1):
                value = jnp.where(spot == m, turned[i + m], value)
            low, high = column - 128 * i, column + n - 128 * i
            if low > 0 or high < 128:
                value = jnp.where((lane >= low) & (lane < high), value, 0.0)
            blocks[target, :] = value[:count]


def split_blocks(blocks, hi, lo):
    def body(t, carry):
        at = pl.multiple_of(t * 16, 16)
        rows = pl.ds(at, 16)
        for i in range(4):
            x = blocks[pl.ds(i * PADDED + at, 16), :]
            h = x.astype(BF16)
            hi[rows, i * 128 : (i + 1) * 128] = h
            lo[rows, i * 128 : (i + 1) * 128] = (x - h.astype(F32)).astype(BF16)
        return carry

    lax.fori_loop(0, PADDED // 16, body, 0)


def pad_order(order, padded):
    lane = lax.broadcasted_iota(jnp.int32, (1, 128), 1)
    for first, n, at, rows in GROUPS:
        for r in range(0, rows, 128):
            block, shift = divmod(first + r, 128)
            value = order[pl.ds(min(block, BLOCKS - 1), 1), :]
            if shift:
                after = order[pl.ds(min(block + 1, BLOCKS - 1), 1), :]
                value = jnp.where(
                    lane < 128 - shift,
                    pltpu.roll(value, 128 - shift, 1),
                    pltpu.roll(after, 128 - shift, 1),
                )
            if r + 128 > n:
                value = jnp.where(lane < n - r, value, -1)
            padded[pl.ds((at + r) // 128, 1), :] = value
    spare = 24 - PADDED_BLOCKS
    padded[pl.ds(PADDED_BLOCKS, spare), :] = jnp.full((spare, 128), -1, jnp.int32)


def invert_order(padded, places):
    total = jnp.zeros((32, 128), F32)
    lane = lax.broadcasted_iota(jnp.int32, (16, 128), 1)
    row = lax.broadcasted_iota(jnp.int32, (16, 128), 0)
    column = lax.broadcasted_iota(jnp.int32, (128, 128), 0)
    for o in range(PADDED_BLOCKS):
        state = padded[pl.ds(o, 1), :]
        place = lane + 128 * o
        for _, n, at, k in GROUPS[1:5]:
            if at <= 128 * o < at + k:
                row_of_block = place - at
                fewest, more = divmod(n, 64)
                slot = row_of_block & 63
                place = (
                    at + slot * fewest + jnp.minimum(slot, more)
                    + lax.shift_right_logical(row_of_block, 6)
                )
        hit = lax.shift_right_arithmetic(state, 7) == row
        left = jnp.concatenate(
            [
                jnp.where(hit, lax.shift_right_logical(place, 4).astype(F32), 0.0),
                jnp.where(hit, (place & 15).astype(F32), 0.0),
            ],
            axis=0,
        ).astype(BF16)
        right = jnp.where((state & 127) == column, 1.0, 0.0).astype(BF16)
        total = total + lax.dot_general(left, right, NT, preferred_element_type=F32)
    places[...] = (16.0 * total[:16] + total[16:]).astype(jnp.int32)


def take(row, index):
    return jnp.take_along_axis(row, index, axis=1, mode="promise_in_bounds")


def tables(orders, gate, top, padded, places, pull, push):
    state = padded[...]
    mapped = jnp.zeros_like(state)
    for t in range(GS):
        mapped = mapped + lax.shift_left(
            lax.shift_right_logical(state, t) & 1, jnp.full_like(state, orders[gate, t])
        )
    if top:
        mapped = (mapped & 3) * 512 + lax.shift_right_logical(mapped, 2)
    pull[...] = jnp.where(state < 0, -1, mapped)
    for half in range(2):
        place = lax.broadcasted_iota(jnp.int32, (8, 128), 0) * 128 + lax.broadcasted_iota(
            jnp.int32, (8, 128), 1
        )
        place = place + half * 1024
        if top:
            place = (place & 511) * 4 + lax.shift_right_logical(place, 9)
        state = jnp.zeros_like(place)
        for t in range(GS):
            bit = lax.shift_right_logical(place, jnp.full_like(place, orders[gate, t])) & 1
            state = state + bit * (1 << t)
        block, lane = lax.shift_right_logical(state, 7), state & 127
        found = jnp.zeros_like(place)
        for i in range(BLOCKS):
            row = jnp.broadcast_to(places[pl.ds(i, 1), :], (8, 128))
            found = jnp.where(block == i, take(row, lane), found)
        push[pl.ds(8 * half, 8), :] = found


def move_block(source, target, table, source_blocks, o):
    index = jnp.broadcast_to(table[pl.ds(o, 1), :], (8, 128))
    block, lane = lax.shift_right_arithmetic(index, 7), index & 127
    hits = [block == i for i in range(source_blocks)]
    for b in range(4):
        found = jnp.zeros((8, 128), F32)
        for i in range(source_blocks):
            piece = source[8 * b : 8 * b + 8, 128 * i : 128 * i + 128]
            found = jnp.where(hits[i], take(piece, lane), found)
        at = o * 128 if isinstance(o, int) else pl.multiple_of(o * 128, 128)
        target[8 * b : 8 * b + 8, pl.ds(at, 128)] = found


def multiply(u, y, hi, lo, at, k):
    x = u[:, at : at + k]
    xh = x.astype(BF16)
    xl = (x - xh.astype(F32)).astype(BF16)
    both = lax.dot_general(
        jnp.concatenate([xh, xl], axis=0), hi[at : at + k, :k], NT, preferred_element_type=F32
    )
    rest = lax.dot_general(xh, lo[at : at + k, :k], NT, preferred_element_type=F32)
    y[:, at : at + k] = both[:32] + both[32:] + rest


def gate(x, u, y, hi, lo, pull, push, ready=None):
    for group, (_, _, at, k) in enumerate(GROUPS):
        for o in range(at // 128, (at + k) // 128):
            move_block(x, u, pull, BLOCKS, o)
        if ready is not None:
            ready(group)
        multiply(u, y, hi, lo, at, k)
    scatter(x, y, push)


def scatter(x, y, push):
    def body(t, carry):
        for step in range(8):
            move_block(y, x, push, PADDED_BLOCKS, t * 8 + step)
        return carry

    lax.fori_loop(0, BLOCKS // 8, body, 0)


def copies_by_group(source, target, sems):
    return [
        pltpu.make_async_copy(
            source.at[pl.ds(at, k), :], target.at[pl.ds(at, k), :], sems.at[group]
        )
        for group, (_, _, at, k) in enumerate(GROUPS)
    ]


def fetch(lo_hbm, lo, sems):
    copies = copies_by_group(lo_hbm, lo, sems)
    for copy in copies:
        copy.start()
    return lambda group: copies[group].wait()


def turn_in(value, at, x):
    turned = value.T
    for g in range(4):
        x[:, 512 * g + at : 512 * g + at + 128] = turned[32 * g : 32 * g + 32]


def top_in(amplitudes, x):
    for at in range(0, 512, 128):
        turn_in(amplitudes[pl.ds(at, 128), :], at, x)


def top_out(x, out):
    for at in range(0, 512, 128):
        pieces = [x[:, 512 * g + at : 512 * g + at + 128] for g in range(4)]
        out[pl.ds(at, 128), :] = jnp.concatenate(pieces, axis=0).T


def low_in(amplitudes, x):
    for g in range(16):
        x[:, 128 * g : 128 * g + 128] = amplitudes[pl.ds(g, 32, stride=16), :]


def low_out(x, out):
    for g in range(16):
        out[pl.ds(g, 32, stride=16), :] = x[:, 128 * g : 128 * g + 128]


def spin(index, position):
    return 1 - 2 * (lax.shift_right_logical(index, position) & 1)


def first_kernel(
    orders, levels, order_hbm, wave_hbm, tail, propagator,
    out, hi, lo_hbm, padded, places,
    flat, blocks, order, wave, lo, x, u, y, pull, push, plain, in_sems, sems,
):
    length = (PROP_ROWS - 1) * 128
    load = pltpu.make_async_copy(
        propagator.at[pl.ds(0, length)],
        flat.reshape(PROP_ROWS * 128).at[pl.ds(0, length)],
        in_sems.at[0],
    )
    load.start()
    order_load = pltpu.make_async_copy(order_hbm, order, in_sems.at[1])
    order_load.start()
    wave_load = pltpu.make_async_copy(wave_hbm, wave, in_sems.at[2])
    wave_load.start()
    device = lax.axis_index("wide") * 8 + lax.axis_index("narrow")
    high = jnp.int32(0)
    for s in range(8):
        high = high + levels[LB + s] * spin(device, s) * spin(device, s + 1)
    border = levels[LB - 1] * spin(device, 0)
    lane = lax.broadcasted_iota(jnp.int32, (8, 128), 1)
    row = lax.broadcasted_iota(jnp.int32, (8, 128), 0)
    spins = [spin(lane, t) for t in range(7)] + [spin(row, t) for t in range(3)]
    common = jnp.zeros((8, 128), jnp.int32) + high
    for t in range(9):
        common = common + levels[t] * (spins[t] * spins[t + 1])
    joined = {z: common + (z * levels[9]) * spins[9] for z in (1, -1)}
    order_load.wait()
    pad_order(order, padded)
    invert_order(padded, places)
    wave_load.wait()
    for at in range(0, 512, 128):
        pieces = []
        for block in range(at // 8, at // 8 + 16):
            z = [1 - 2 * (block >> t & 1) for t in range(6)]
            rest = border * z[5]
            for t in range(5):
                rest = rest + levels[10 + t] * (z[t] * z[t + 1])
            energy = joined[z[0]] + rest
            pieces.append(
                wave[pl.ds(8 * block, 8), :] * jnp.exp(-ZZ_RATE * energy.astype(F32))
            )
        turn_in(jnp.concatenate(pieces, axis=0), at, x)
    load.wait()
    flat[pl.ds(PROP_ROWS - 1, 1), :] = tail[...]
    lay_out_blocks(flat, blocks)
    split_blocks(blocks, hi, lo)
    saves = copies_by_group(lo, lo_hbm, sems)
    for copy in saves:
        copy.start()
    rest = (x, u, y, hi, lo, pull, push)
    tables(orders, 0, True, padded, places, pull, push)
    gate(*rest)
    top_out(x, plain)
    low_in(plain, x)
    tables(orders, 1, False, padded, places, pull, push)
    gate(*rest)
    low_out(x, out)
    for copy in saves:
        copy.wait()


def tables_kernel(orders, padded, places, pull, push):
    for i, number in enumerate((2, 3, 4, 5)):
        tables(orders, number, number in (2, 4), padded, places, pull.at[i], push.at[i])


def second_kernel(amplitudes, pull, push, hi, lo_hbm, out, lo, x, u, y, sems):
    ready = fetch(lo_hbm, lo, sems)
    top_in(amplitudes, x)
    gate(x, u, y, hi, lo, pull.at[0], push.at[0], ready)
    top_out(x, out)


def third_kernel(amplitudes, pull, push, hi, lo_hbm, out, lo, x, u, y, plain, sems):
    ready = fetch(lo_hbm, lo, sems)
    low_in(amplitudes, x)
    gate(x, u, y, hi, lo, pull.at[1], push.at[1], ready)
    low_out(x, plain)
    top_in(plain, x)
    gate(x, u, y, hi, lo, pull.at[2], push.at[2])
    top_out(x, plain)
    low_in(plain, x)
    gate(x, u, y, hi, lo, pull.at[3], push.at[3])
    low_out(x, out)


SMEM = pl.BlockSpec(memory_space=pltpu.SMEM)
VMEM = pl.BlockSpec(memory_space=pltpu.VMEM)
HBM = pl.BlockSpec(memory_space=pltpu.HBM)
AMPLITUDES = jax.ShapeDtypeStruct((512, 128), F32)
HALF = pltpu.VMEM((PADDED, 512), BF16)
GRANT = pltpu.CompilerParams(vmem_limit_bytes=24 << 20)
SCRATCH = [
    HALF,
    pltpu.VMEM((32, STATES), F32),
    pltpu.VMEM((32, PADDED), F32),
    pltpu.VMEM((32, PADDED), F32),
]
TABLES = [pltpu.VMEM((24, 128), jnp.int32), pltpu.VMEM((16, 128), jnp.int32)]
PLAIN = pltpu.VMEM((512, 128), F32)
SEMS = pltpu.SemaphoreType.DMA((6,))


def in_hbm(array):
    return pltpu.with_memory_space_constraint(array, pltpu.HBM)


def exchange(amplitudes):
    return lax.all_to_all(amplitudes, ("narrow", "wide"), split_axis=0, concat_axis=0, tiled=True)


def shards(wavefunction, propagator, gate_orders, sector_order, bond_level):
    length = (PROP_ROWS - 1) * 128
    spare = PROP_ROWS * 128 - propagator.shape[0]
    tail = lax.pad(propagator, jnp.float32(0), [(-length, spare, 0)]).reshape(1, 128)
    amplitudes, hi, lo, padded, places = pl.pallas_call(
        first_kernel,
        out_shape=(
            AMPLITUDES,
            HALF,
            pltpu.HBM((PADDED, 512), BF16),
            jax.ShapeDtypeStruct((24, 128), jnp.int32),
            jax.ShapeDtypeStruct((16, 128), jnp.int32),
        ),
        in_specs=[SMEM, SMEM, HBM, HBM, VMEM, HBM],
        out_specs=(VMEM, VMEM, HBM, VMEM, VMEM),
        scratch_shapes=[
            pltpu.VMEM((PROP_ROWS, 128), F32),
            pltpu.VMEM((4 * PADDED, 128), F32),
            pltpu.VMEM((16, 128), jnp.int32),
            PLAIN,
            *SCRATCH,
            *TABLES,
            PLAIN,
            pltpu.SemaphoreType.DMA((3,)),
            SEMS,
        ],
        compiler_params=GRANT,
        name="first",
    )(
        gate_orders,
        bond_level,
        in_hbm(sector_order.reshape(16, 128)),
        in_hbm(wavefunction.reshape(512, 128)),
        tail,
        in_hbm(propagator),
    )
    lo = in_hbm(lo)
    amplitudes = exchange(amplitudes)
    pull, push = pl.pallas_call(
        tables_kernel,
        out_shape=(
            jax.ShapeDtypeStruct((4, 24, 128), jnp.int32),
            jax.ShapeDtypeStruct((4, 16, 128), jnp.int32),
        ),
        in_specs=[SMEM, VMEM, VMEM],
        out_specs=(VMEM, VMEM),
        compiler_params=GRANT,
        name="tables",
    )(gate_orders, padded, places)
    amplitudes = pl.pallas_call(
        second_kernel,
        out_shape=AMPLITUDES,
        in_specs=[VMEM, VMEM, VMEM, VMEM, HBM],
        out_specs=VMEM,
        scratch_shapes=[*SCRATCH, SEMS],
        compiler_params=GRANT,
        name="second",
    )(amplitudes, pull, push, hi, lo)
    amplitudes = exchange(amplitudes)
    amplitudes = pl.pallas_call(
        third_kernel,
        out_shape=AMPLITUDES,
        in_specs=[VMEM, VMEM, VMEM, VMEM, HBM],
        out_specs=VMEM,
        scratch_shapes=[*SCRATCH, PLAIN, SEMS],
        compiler_params=GRANT,
        name="third",
    )(amplitudes, pull, push, hi, lo)
    return amplitudes.reshape(-1)


def solution(mesh):
    in_specs = (P(("wide", "narrow")), P(), P(), P(), P())
    out_specs = P(("wide", "narrow"))
    return jax.shard_map(shards, mesh=mesh, in_specs=in_specs, out_specs=out_specs, check_vma=False)
```

```python
import math

import jax
import jax.numpy as jnp
from jax import lax
from jax.experimental import pallas as pl
from jax.experimental.pallas import tpu as pltpu
from jax.sharding import PartitionSpec as P

LB = 16
GS = 11
STATES = 2048
ZZ_RATE = 0.06
F32 = jnp.float32
BF16 = jnp.bfloat16

SIZES = [math.comb(GS, k) for k in range(GS + 1)]
PROP_ROWS = 5512
NT = (((1,), (1,)), ((), ()))
GROUPS = [
    (0, 232, 0, 256),
    (232, 330, 256, 384),
    (562, 462, 640, 512),
    (1024, 462, 1152, 512),
    (1486, 330, 1664, 384),
    (1816, 232, 2048, 256),
]
PADDED = 2304
PADDED_BLOCKS = PADDED // 128
BLOCKS = STATES // 128


def lay_out_blocks(flat, blocks):
    starts = []
    at = 0
    for n in SIZES:
        starts.append(at)
        at += n * n
    lane = lax.broadcasted_iota(jnp.int32, (8, 128), 1)

    def shifted(piece_of, count, shift, columns):
        pieces = []
        for i in range(columns + (1 if shift else 0)):
            piece = piece_of(i)
            pieces.append(pltpu.roll(piece, 128 - shift, 1) if shift else piece)
        if not shift:
            return pieces
        keep = lane[:count] < 128 - shift
        return [jnp.where(keep, pieces[i], pieces[i + 1]) for i in range(columns)]

    for degree, group in ((4, 1), (5, 2), (6, 3), (7, 4)):
        n = SIZES[degree]
        row0 = GROUPS[group][2]
        columns = -(-n // 128)
        step = n // 2
        placed = row0
        for s in range(64):
            count = len(range(s, n, 64))
            first, shift = divmod(starts[degree] + n * s, 128)
            rows = shifted(
                lambda i: flat[pl.ds(first + i, count, stride=step), :], count, shift, columns
            )
            for i in range(columns):
                blocks[pl.ds(i * PADDED + placed, count), :] = rows[i]
            placed += count
    for group, degrees in ((0, (0, 1, 2, 3)), (5, (8, 9, 10, 11))):
        row0 = GROUPS[group][2]
        column = 0
        for degree in degrees:
            small_sector(flat, blocks, starts[degree], SIZES[degree], row0, column)
            column += SIZES[degree]


def small_sector(flat, blocks, start, n, row0, column):
    lane = lax.broadcasted_iota(jnp.int32, (8, 128), 1)
    row = lax.broadcasted_iota(jnp.int32, (8, 128), 0)
    step, extra = divmod(n, 128)
    sides = [i for i in range(2) if max(column, 128 * i) < min(column + n, 128 * i + 128)]
    for r in range(0, n, 8):
        count = min(8, n - r)
        first, shift = divmod(start + n * r - column, 128)
        spot = lane + (row * extra + shift)
        from_lane = spot & 127
        spot = lax.shift_right_logical(spot, 7)
        last = (shift + extra * (count - 1) + 127) >> 7
        turned = {}
        for m in range(min(sides), max(sides) + last + 1):
            if step:
                at = min(first + m, PROP_ROWS - 8)
                piece = flat[pl.ds(at, 8), :]
            else:
                at = min(first + m, PROP_ROWS - 1)
                piece = jnp.broadcast_to(flat[pl.ds(at, 1), :], (8, 128))
            turned[m] = take(piece, from_lane)
        for i in range(2):
            target = pl.ds(i * PADDED + row0 + column + r, count)
            if i not in sides:
                blocks[target, :] = jnp.zeros((count, 128), F32)
                continue
            value = turned[i]
            for m in range(1, last + 1):
                value = jnp.where(spot == m, turned[i + m], value)
            low, high = column - 128 * i, column + n - 128 * i
            if low > 0 or high < 128:
                value = jnp.where((lane >= low) & (lane < high), value, 0.0)
            blocks[target, :] = value[:count]


def split_blocks(blocks, hi, lo):
    def body(t, carry):
        at = pl.multiple_of(t * 16, 16)
        rows = pl.ds(at, 16)
        for i in range(4):
            x = blocks[pl.ds(i * PADDED + at, 16), :]
            h = x.astype(BF16)
            hi[rows, i * 128 : (i + 1) * 128] = h
            lo[rows, i * 128 : (i + 1) * 128] = (x - h.astype(F32)).astype(BF16)
        return carry

    lax.fori_loop(0, PADDED // 16, body, 0)


def pad_order(order, padded):
    lane = lax.broadcasted_iota(jnp.int32, (1, 128), 1)
    for first, n, at, rows in GROUPS:
        for r in range(0, rows, 128):
            block, shift = divmod(first + r, 128)
            value = order[pl.ds(min(block, BLOCKS - 1), 1), :]
            if shift:
                after = order[pl.ds(min(block + 1, BLOCKS - 1), 1), :]
                value = jnp.where(
                    lane < 128 - shift,
                    pltpu.roll(value, 128 - shift, 1),
                    pltpu.roll(after, 128 - shift, 1),
                )
            if r + 128 > n:
                value = jnp.where(lane < n - r, value, -1)
            padded[pl.ds((at + r) // 128, 1), :] = value
    spare = 24 - PADDED_BLOCKS
    padded[pl.ds(PADDED_BLOCKS, spare), :] = jnp.full((spare, 128), -1, jnp.int32)


def invert_order(padded, places):
    total = jnp.zeros((32, 128), F32)
    lane = lax.broadcasted_iota(jnp.int32, (16, 128), 1)
    row = lax.broadcasted_iota(jnp.int32, (16, 128), 0)
    column = lax.broadcasted_iota(jnp.int32, (128, 128), 0)
    for o in range(PADDED_BLOCKS):
        state = padded[pl.ds(o, 1), :]
        place = lane + 128 * o
        for _, n, at, k in GROUPS[1:5]:
            if at <= 128 * o < at + k:
                row_of_block = place - at
                fewest, more = divmod(n, 64)
                slot = row_of_block & 63
                place = (
                    at + slot * fewest + jnp.minimum(slot, more)
                    + lax.shift_right_logical(row_of_block, 6)
                )
        hit = lax.shift_right_arithmetic(state, 7) == row
        left = jnp.concatenate(
            [
                jnp.where(hit, lax.shift_right_logical(place, 4).astype(F32), 0.0),
                jnp.where(hit, (place & 15).astype(F32), 0.0),
            ],
            axis=0,
        ).astype(BF16)
        right = jnp.where((state & 127) == column, 1.0, 0.0).astype(BF16)
        total = total + lax.dot_general(left, right, NT, preferred_element_type=F32)
    places[...] = (16.0 * total[:16] + total[16:]).astype(jnp.int32)


def take(row, index):
    return jnp.take_along_axis(row, index, axis=1, mode="promise_in_bounds")


def tables(orders, gate, top, padded, places, pull, push):
    state = padded[...]
    mapped = jnp.zeros_like(state)
    for t in range(GS):
        mapped = mapped + lax.shift_left(
            lax.shift_right_logical(state, t) & 1, jnp.full_like(state, orders[gate, t])
        )
    if top:
        mapped = (mapped & 3) * 512 + lax.shift_right_logical(mapped, 2)
    pull[...] = jnp.where(state < 0, -1, mapped)
    for half in range(2):
        place = lax.broadcasted_iota(jnp.int32, (8, 128), 0) * 128 + lax.broadcasted_iota(
            jnp.int32, (8, 128), 1
        )
        place = place + half * 1024
        if top:
            place = (place & 511) * 4 + lax.shift_right_logical(place, 9)
        state = jnp.zeros_like(place)
        for t in range(GS):
            bit = lax.shift_right_logical(place, jnp.full_like(place, orders[gate, t])) & 1
            state = state + bit * (1 << t)
        block, lane = lax.shift_right_logical(state, 7), state & 127
        found = jnp.zeros_like(place)
        for i in range(BLOCKS):
            row = jnp.broadcast_to(places[pl.ds(i, 1), :], (8, 128))
            found = jnp.where(block == i, take(row, lane), found)
        push[pl.ds(8 * half, 8), :] = found


def move_block(source, target, table, source_blocks, o):
    index = jnp.broadcast_to(table[pl.ds(o, 1), :], (8, 128))
    block, lane = lax.shift_right_arithmetic(index, 7), index & 127
    hits = [block == i for i in range(source_blocks)]
    for b in range(4):
        found = jnp.zeros((8, 128), F32)
        for i in range(source_blocks):
            piece = source[8 * b : 8 * b + 8, 128 * i : 128 * i + 128]
            found = jnp.where(hits[i], take(piece, lane), found)
        at = o * 128 if isinstance(o, int) else pl.multiple_of(o * 128, 128)
        target[8 * b : 8 * b + 8, pl.ds(at, 128)] = found


def multiply(u, y, hi, lo, at, k):
    x = u[:, at : at + k]
    xh = x.astype(BF16)
    xl = (x - xh.astype(F32)).astype(BF16)
    both = lax.dot_general(
        jnp.concatenate([xh, xl], axis=0), hi[at : at + k, :k], NT, preferred_element_type=F32
    )
    rest = lax.dot_general(xh, lo[at : at + k, :k], NT, preferred_element_type=F32)
    y[:, at : at + k] = both[:32] + both[32:] + rest


def gate(x, u, y, hi, lo, pull, push):
    for _, _, at, k in GROUPS:
        for o in range(at // 128, (at + k) // 128):
            move_block(x, u, pull, BLOCKS, o)
        multiply(u, y, hi, lo, at, k)
    scatter(x, y, push)


def scatter(x, y, push):
    def body(t, carry):
        for step in range(8):
            move_block(y, x, push, PADDED_BLOCKS, t * 8 + step)
        return carry

    lax.fori_loop(0, BLOCKS // 8, body, 0)


def turn_in(value, at, x):
    turned = value.T
    for g in range(4):
        x[:, 512 * g + at : 512 * g + at + 128] = turned[32 * g : 32 * g + 32]


def top_in(amplitudes, x):
    for at in range(0, 512, 128):
        turn_in(amplitudes[pl.ds(at, 128), :], at, x)


def top_out(x, out):
    for at in range(0, 512, 128):
        pieces = [x[:, 512 * g + at : 512 * g + at + 128] for g in range(4)]
        out[pl.ds(at, 128), :] = jnp.concatenate(pieces, axis=0).T


def low_in(amplitudes, x):
    for g in range(16):
        x[:, 128 * g : 128 * g + 128] = amplitudes[pl.ds(g, 32, stride=16), :]


def low_out(x, out):
    for g in range(16):
        out[pl.ds(g, 32, stride=16), :] = x[:, 128 * g : 128 * g + 128]


def spin(index, position):
    return 1 - 2 * (lax.shift_right_logical(index, position) & 1)


def first_kernel(
    orders, levels, order_hbm, wave_hbm, tail, propagator,
    out, hi, lo, pulls, pushes,
    flat, blocks, order, wave, padded, places, x, u, y, pull, push, plain, in_sems,
):
    length = (PROP_ROWS - 1) * 128
    load = pltpu.make_async_copy(
        propagator.at[pl.ds(0, length)],
        flat.reshape(PROP_ROWS * 128).at[pl.ds(0, length)],
        in_sems.at[0],
    )
    load.start()
    order_load = pltpu.make_async_copy(order_hbm, order, in_sems.at[1])
    order_load.start()
    wave_load = pltpu.make_async_copy(wave_hbm, wave, in_sems.at[2])
    wave_load.start()
    device = lax.axis_index("wide") * 8 + lax.axis_index("narrow")
    high = jnp.int32(0)
    for s in range(8):
        high = high + levels[LB + s] * spin(device, s) * spin(device, s + 1)
    border = levels[LB - 1] * spin(device, 0)
    lane = lax.broadcasted_iota(jnp.int32, (8, 128), 1)
    row = lax.broadcasted_iota(jnp.int32, (8, 128), 0)
    spins = [spin(lane, t) for t in range(7)] + [spin(row, t) for t in range(3)]
    common = jnp.zeros((8, 128), jnp.int32) + high
    for t in range(9):
        common = common + levels[t] * (spins[t] * spins[t + 1])
    joined = {z: common + (z * levels[9]) * spins[9] for z in (1, -1)}
    order_load.wait()
    pad_order(order, padded)
    invert_order(padded, places)
    wave_load.wait()
    for at in range(0, 512, 128):
        pieces = []
        for block in range(at // 8, at // 8 + 16):
            z = [1 - 2 * (block >> t & 1) for t in range(6)]
            rest = border * z[5]
            for t in range(5):
                rest = rest + levels[10 + t] * (z[t] * z[t + 1])
            energy = joined[z[0]] + rest
            pieces.append(
                wave[pl.ds(8 * block, 8), :] * jnp.exp(-ZZ_RATE * energy.astype(F32))
            )
        turn_in(jnp.concatenate(pieces, axis=0), at, x)
    load.wait()
    flat[pl.ds(PROP_ROWS - 1, 1), :] = tail[...]
    lay_out_blocks(flat, blocks)
    split_blocks(blocks, hi, lo)
    rest = (x, u, y, hi, lo, pull, push)
    tables(orders, 0, True, padded, places, pull, push)
    gate(*rest)
    top_out(x, plain)
    low_in(plain, x)
    tables(orders, 1, False, padded, places, pull, push)
    gate(*rest)
    low_out(x, out)
    for i, number in enumerate((2, 3, 4, 5)):
        tables(orders, number, number in (2, 4), padded, places, pulls.at[i], pushes.at[i])


def second_kernel(amplitudes, pull, push, hi, lo, out, x, u, y):
    top_in(amplitudes, x)
    gate(x, u, y, hi, lo, pull.at[0], push.at[0])
    top_out(x, out)


def third_kernel(amplitudes, pull, push, hi, lo, out, x, u, y, plain):
    low_in(amplitudes, x)
    gate(x, u, y, hi, lo, pull.at[1], push.at[1])
    low_out(x, plain)
    top_in(plain, x)
    gate(x, u, y, hi, lo, pull.at[2], push.at[2])
    top_out(x, plain)
    low_in(plain, x)
    gate(x, u, y, hi, lo, pull.at[3], push.at[3])
    low_out(x, out)


SMEM = pl.BlockSpec(memory_space=pltpu.SMEM)
VMEM = pl.BlockSpec(memory_space=pltpu.VMEM)
HBM = pl.BlockSpec(memory_space=pltpu.HBM)
AMPLITUDES = jax.ShapeDtypeStruct((512, 128), F32)
HALF = pltpu.VMEM((PADDED, 512), BF16)
GRANT = pltpu.CompilerParams(vmem_limit_bytes=24 << 20)
SCRATCH = [
    pltpu.VMEM((32, STATES), F32),
    pltpu.VMEM((32, PADDED), F32),
    pltpu.VMEM((32, PADDED), F32),
]
TABLES = [pltpu.VMEM((24, 128), jnp.int32), pltpu.VMEM((16, 128), jnp.int32)]
PLAIN = pltpu.VMEM((512, 128), F32)


def in_hbm(array):
    return pltpu.with_memory_space_constraint(array, pltpu.HBM)


def exchange(amplitudes):
    return lax.all_to_all(amplitudes, ("narrow", "wide"), split_axis=0, concat_axis=0, tiled=True)


def shards(wavefunction, propagator, gate_orders, sector_order, bond_level):
    length = (PROP_ROWS - 1) * 128
    spare = PROP_ROWS * 128 - propagator.shape[0]
    tail = lax.pad(propagator, jnp.float32(0), [(-length, spare, 0)]).reshape(1, 128)
    amplitudes, hi, lo, pull, push = pl.pallas_call(
        first_kernel,
        out_shape=(
            AMPLITUDES,
            HALF,
            HALF,
            jax.ShapeDtypeStruct((4, 24, 128), jnp.int32),
            jax.ShapeDtypeStruct((4, 16, 128), jnp.int32),
        ),
        in_specs=[SMEM, SMEM, HBM, HBM, VMEM, HBM],
        out_specs=(VMEM,) * 5,
        scratch_shapes=[
            pltpu.VMEM((PROP_ROWS, 128), F32),
            pltpu.VMEM((4 * PADDED, 128), F32),
            pltpu.VMEM((16, 128), jnp.int32),
            PLAIN,
            pltpu.VMEM((24, 128), jnp.int32),
            pltpu.VMEM((16, 128), jnp.int32),
            *SCRATCH,
            *TABLES,
            PLAIN,
            pltpu.SemaphoreType.DMA((3,)),
        ],
        compiler_params=GRANT,
        name="first",
    )(
        gate_orders,
        bond_level,
        in_hbm(sector_order.reshape(16, 128)),
        in_hbm(wavefunction.reshape(512, 128)),
        tail,
        in_hbm(propagator),
    )
    amplitudes = exchange(amplitudes)
    amplitudes = pl.pallas_call(
        second_kernel,
        out_shape=AMPLITUDES,
        in_specs=[VMEM] * 5,
        out_specs=VMEM,
        scratch_shapes=SCRATCH,
        compiler_params=GRANT,
        name="second",
    )(amplitudes, pull, push, hi, lo)
    amplitudes = exchange(amplitudes)
    amplitudes = pl.pallas_call(
        third_kernel,
        out_shape=AMPLITUDES,
        in_specs=[VMEM] * 5,
        out_specs=VMEM,
        scratch_shapes=[*SCRATCH, PLAIN],
        compiler_params=GRANT,
        name="third",
    )(amplitudes, pull, push, hi, lo)
    return amplitudes.reshape(-1)


def solution(mesh):
    in_specs = (P(("wide", "narrow")), P(), P(), P(), P())
    out_specs = P(("wide", "narrow"))
    return jax.shard_map(shards, mesh=mesh, in_specs=in_specs, out_specs=out_specs, check_vma=False)
```

```python
import math

import jax
import jax.numpy as jnp
from jax import lax
from jax.experimental import pallas as pl
from jax.experimental.pallas import tpu as pltpu
from jax.sharding import PartitionSpec as P

LB = 16
GS = 11
STATES = 2048
ZZ_RATE = 0.06
F32 = jnp.float32
BF16 = jnp.bfloat16

SIZES = [math.comb(GS, k) for k in range(GS + 1)]
PROP_ROWS = 5512
NT = (((1,), (1,)), ((), ()))
GROUPS = [
    (0, 232, 0, 256),
    (232, 330, 256, 384),
    (562, 462, 640, 512),
    (1024, 462, 1152, 512),
    (1486, 330, 1664, 384),
    (1816, 232, 2048, 256),
]
PADDED = 2304
PADDED_BLOCKS = PADDED // 128
BLOCKS = STATES // 128


def lay_out_blocks(flat, blocks):
    starts = []
    at = 0
    for n in SIZES:
        starts.append(at)
        at += n * n
    lane = lax.broadcasted_iota(jnp.int32, (8, 128), 1)

    def shifted(piece_of, count, shift, columns):
        pieces = []
        for i in range(columns + (1 if shift else 0)):
            piece = piece_of(i)
            pieces.append(pltpu.roll(piece, 128 - shift, 1) if shift else piece)
        if not shift:
            return pieces
        keep = lane[:count] < 128 - shift
        return [jnp.where(keep, pieces[i], pieces[i + 1]) for i in range(columns)]

    for degree, group in ((4, 1), (5, 2), (6, 3), (7, 4)):
        n = SIZES[degree]
        row0 = GROUPS[group][2]
        columns = -(-n // 128)
        step = n // 2
        placed = row0
        for s in range(64):
            count = len(range(s, n, 64))
            first, shift = divmod(starts[degree] + n * s, 128)
            rows = shifted(
                lambda i: flat[pl.ds(first + i, count, stride=step), :], count, shift, columns
            )
            for i in range(columns):
                blocks[pl.ds(i * PADDED + placed, count), :] = rows[i]
            placed += count
    for group, degrees in ((0, (0, 1, 2, 3)), (5, (8, 9, 10, 11))):
        row0 = GROUPS[group][2]
        column = 0
        for degree in degrees:
            small_sector(flat, blocks, starts[degree], SIZES[degree], row0, column)
            column += SIZES[degree]


def small_sector(flat, blocks, start, n, row0, column):
    lane = lax.broadcasted_iota(jnp.int32, (8, 128), 1)
    row = lax.broadcasted_iota(jnp.int32, (8, 128), 0)
    step, extra = divmod(n, 128)
    sides = [i for i in range(2) if max(column, 128 * i) < min(column + n, 128 * i + 128)]
    for r in range(0, n, 8):
        count = min(8, n - r)
        first, shift = divmod(start + n * r - column, 128)
        spot = lane + (row * extra + shift)
        from_lane = spot & 127
        spot = lax.shift_right_logical(spot, 7)
        last = (shift + extra * (count - 1) + 127) >> 7
        turned = {}
        for m in range(min(sides), max(sides) + last + 1):
            if step:
                at = min(first + m, PROP_ROWS - 8)
                piece = flat[pl.ds(at, 8), :]
            else:
                at = min(first + m, PROP_ROWS - 1)
                piece = jnp.broadcast_to(flat[pl.ds(at, 1), :], (8, 128))
            turned[m] = take(piece, from_lane)
        for i in range(2):
            target = pl.ds(i * PADDED + row0 + column + r, count)
            if i not in sides:
                blocks[target, :] = jnp.zeros((count, 128), F32)
                continue
            value = turned[i]
            for m in range(1, last + 1):
                value = jnp.where(spot == m, turned[i + m], value)
            low, high = column - 128 * i, column + n - 128 * i
            if low > 0 or high < 128:
                value = jnp.where((lane >= low) & (lane < high), value, 0.0)
            blocks[target, :] = value[:count]


def split_blocks(blocks, hi, lo):
    def body(t, carry):
        at = pl.multiple_of(t * 16, 16)
        rows = pl.ds(at, 16)
        for i in range(4):
            x = blocks[pl.ds(i * PADDED + at, 16), :]
            h = x.astype(BF16)
            hi[rows, i * 128 : (i + 1) * 128] = h
            lo[rows, i * 128 : (i + 1) * 128] = (x - h.astype(F32)).astype(BF16)
        return carry

    lax.fori_loop(0, PADDED // 16, body, 0)


def pad_order(order, padded):
    lane = lax.broadcasted_iota(jnp.int32, (1, 128), 1)
    for first, n, at, rows in GROUPS:
        for r in range(0, rows, 128):
            block, shift = divmod(first + r, 128)
            value = order[pl.ds(min(block, BLOCKS - 1), 1), :]
            if shift:
                after = order[pl.ds(min(block + 1, BLOCKS - 1), 1), :]
                value = jnp.where(
                    lane < 128 - shift,
                    pltpu.roll(value, 128 - shift, 1),
                    pltpu.roll(after, 128 - shift, 1),
                )
            if r + 128 > n:
                value = jnp.where(lane < n - r, value, -1)
            padded[pl.ds((at + r) // 128, 1), :] = value
    spare = 24 - PADDED_BLOCKS
    padded[pl.ds(PADDED_BLOCKS, spare), :] = jnp.full((spare, 128), -1, jnp.int32)


def invert_order(padded, places):
    total = jnp.zeros((32, 128), F32)
    lane = lax.broadcasted_iota(jnp.int32, (16, 128), 1)
    row = lax.broadcasted_iota(jnp.int32, (16, 128), 0)
    column = lax.broadcasted_iota(jnp.int32, (128, 128), 0)
    for o in range(PADDED_BLOCKS):
        state = padded[pl.ds(o, 1), :]
        place = lane + 128 * o
        for _, n, at, k in GROUPS[1:5]:
            if at <= 128 * o < at + k:
                row_of_block = place - at
                fewest, more = divmod(n, 64)
                slot = row_of_block & 63
                place = (
                    at + slot * fewest + jnp.minimum(slot, more)
                    + lax.shift_right_logical(row_of_block, 6)
                )
        hit = lax.shift_right_arithmetic(state, 7) == row
        left = jnp.concatenate(
            [
                jnp.where(hit, lax.shift_right_logical(place, 4).astype(F32), 0.0),
                jnp.where(hit, (place & 15).astype(F32), 0.0),
            ],
            axis=0,
        ).astype(BF16)
        right = jnp.where((state & 127) == column, 1.0, 0.0).astype(BF16)
        total = total + lax.dot_general(left, right, NT, preferred_element_type=F32)
    places[...] = (16.0 * total[:16] + total[16:]).astype(jnp.int32)


def take(row, index):
    return jnp.take_along_axis(row, index, axis=1, mode="promise_in_bounds")


def tables(orders, gate, top, padded, places, pull, push):
    state = padded[...]
    mapped = jnp.zeros_like(state)
    for t in range(GS):
        mapped = mapped + lax.shift_left(
            lax.shift_right_logical(state, t) & 1, jnp.full_like(state, orders[gate, t])
        )
    if top:
        mapped = (mapped & 3) * 512 + lax.shift_right_logical(mapped, 2)
    pull[...] = jnp.where(state < 0, -1, mapped)
    for half in range(2):
        place = lax.broadcasted_iota(jnp.int32, (8, 128), 0) * 128 + lax.broadcasted_iota(
            jnp.int32, (8, 128), 1
        )
        place = place + half * 1024
        if top:
            place = (place & 511) * 4 + lax.shift_right_logical(place, 9)
        state = jnp.zeros_like(place)
        for t in range(GS):
            bit = lax.shift_right_logical(place, jnp.full_like(place, orders[gate, t])) & 1
            state = state + bit * (1 << t)
        block, lane = lax.shift_right_logical(state, 7), state & 127
        found = jnp.zeros_like(place)
        for i in range(BLOCKS):
            row = jnp.broadcast_to(places[pl.ds(i, 1), :], (8, 128))
            found = jnp.where(block == i, take(row, lane), found)
        push[pl.ds(8 * half, 8), :] = found


def move_block(source, target, table, source_blocks, o):
    index = jnp.broadcast_to(table[pl.ds(o, 1), :], (8, 128))
    block, lane = lax.shift_right_arithmetic(index, 7), index & 127
    hits = [block == i for i in range(source_blocks)]
    for b in range(4):
        found = jnp.zeros((8, 128), F32)
        for i in range(source_blocks):
            piece = source[8 * b : 8 * b + 8, 128 * i : 128 * i + 128]
            found = jnp.where(hits[i], take(piece, lane), found)
        at = o * 128 if isinstance(o, int) else pl.multiple_of(o * 128, 128)
        target[8 * b : 8 * b + 8, pl.ds(at, 128)] = found


def multiply(u, y, hi, lo, at, k):
    x = u[:, at : at + k]
    xh = x.astype(BF16)
    xl = (x - xh.astype(F32)).astype(BF16)
    both = lax.dot_general(
        jnp.concatenate([xh, xl], axis=0), hi[at : at + k, :k], NT, preferred_element_type=F32
    )
    rest = lax.dot_general(xh, lo[at : at + k, :k], NT, preferred_element_type=F32)
    y[:, at : at + k] = both[:32] + both[32:] + rest


def gate(x, u, y, hi, lo, pull, push):
    for _, _, at, k in GROUPS:
        for o in range(at // 128, (at + k) // 128):
            move_block(x, u, pull, BLOCKS, o)
        multiply(u, y, hi, lo, at, k)
    scatter(x, y, push)


def scatter(x, y, push):
    for o in range(BLOCKS):
        move_block(y, x, push, PADDED_BLOCKS, o)


def turn_in(value, at, x):
    turned = value.T
    for g in range(4):
        x[:, 512 * g + at : 512 * g + at + 128] = turned[32 * g : 32 * g + 32]


def top_in(amplitudes, x):
    for at in range(0, 512, 128):
        turn_in(amplitudes[pl.ds(at, 128), :], at, x)


def top_out(x, out):
    for at in range(0, 512, 128):
        pieces = [x[:, 512 * g + at : 512 * g + at + 128] for g in range(4)]
        out[pl.ds(at, 128), :] = jnp.concatenate(pieces, axis=0).T


def low_in(amplitudes, x):
    for g in range(16):
        x[:, 128 * g : 128 * g + 128] = amplitudes[pl.ds(g, 32, stride=16), :]


def low_out(x, out):
    for g in range(16):
        out[pl.ds(g, 32, stride=16), :] = x[:, 128 * g : 128 * g + 128]


def spin(index, position):
    return 1 - 2 * (lax.shift_right_logical(index, position) & 1)


def first_kernel(
    orders, levels, order_hbm, wave_hbm, tail, propagator,
    out, hi, lo, pulls, pushes,
    flat, blocks, order, wave, padded, places, x, u, y, pull, push, plain, in_sems,
):
    length = (PROP_ROWS - 1) * 128
    load = pltpu.make_async_copy(
        propagator.at[pl.ds(0, length)],
        flat.reshape(PROP_ROWS * 128).at[pl.ds(0, length)],
        in_sems.at[0],
    )
    load.start()
    order_load = pltpu.make_async_copy(order_hbm, order, in_sems.at[1])
    order_load.start()
    wave_load = pltpu.make_async_copy(wave_hbm, wave, in_sems.at[2])
    wave_load.start()
    device = lax.axis_index("wide") * 8 + lax.axis_index("narrow")
    high = jnp.int32(0)
    for s in range(8):
        high = high + levels[LB + s] * spin(device, s) * spin(device, s + 1)
    border = levels[LB - 1] * spin(device, 0)
    lane = lax.broadcasted_iota(jnp.int32, (8, 128), 1)
    row = lax.broadcasted_iota(jnp.int32, (8, 128), 0)
    spins = [spin(lane, t) for t in range(7)] + [spin(row, t) for t in range(3)]
    common = jnp.zeros((8, 128), jnp.int32) + high
    for t in range(9):
        common = common + levels[t] * (spins[t] * spins[t + 1])
    joined = {z: common + (z * levels[9]) * spins[9] for z in (1, -1)}
    order_load.wait()
    pad_order(order, padded)
    invert_order(padded, places)
    wave_load.wait()
    for at in range(0, 512, 128):
        pieces = []
        for block in range(at // 8, at // 8 + 16):
            z = [1 - 2 * (block >> t & 1) for t in range(6)]
            rest = border * z[5]
            for t in range(5):
                rest = rest + levels[10 + t] * (z[t] * z[t + 1])
            energy = joined[z[0]] + rest
            pieces.append(
                wave[pl.ds(8 * block, 8), :] * jnp.exp(-ZZ_RATE * energy.astype(F32))
            )
        turn_in(jnp.concatenate(pieces, axis=0), at, x)
    load.wait()
    flat[pl.ds(PROP_ROWS - 1, 1), :] = tail[...]
    lay_out_blocks(flat, blocks)
    split_blocks(blocks, hi, lo)
    rest = (x, u, y, hi, lo, pull, push)
    tables(orders, 0, True, padded, places, pull, push)
    gate(*rest)
    top_out(x, plain)
    low_in(plain, x)
    tables(orders, 1, False, padded, places, pull, push)
    gate(*rest)
    low_out(x, out)
    for i, number in enumerate((2, 3, 4, 5)):
        tables(orders, number, number in (2, 4), padded, places, pulls.at[i], pushes.at[i])


def second_kernel(amplitudes, pull, push, hi, lo, out, x, u, y):
    top_in(amplitudes, x)
    gate(x, u, y, hi, lo, pull.at[0], push.at[0])
    top_out(x, out)


def third_kernel(amplitudes, pull, push, hi, lo, out, x, u, y, plain):
    low_in(amplitudes, x)
    gate(x, u, y, hi, lo, pull.at[1], push.at[1])
    low_out(x, plain)
    top_in(plain, x)
    gate(x, u, y, hi, lo, pull.at[2], push.at[2])
    top_out(x, plain)
    low_in(plain, x)
    gate(x, u, y, hi, lo, pull.at[3], push.at[3])
    low_out(x, out)


SMEM = pl.BlockSpec(memory_space=pltpu.SMEM)
VMEM = pl.BlockSpec(memory_space=pltpu.VMEM)
HBM = pl.BlockSpec(memory_space=pltpu.HBM)
AMPLITUDES = jax.ShapeDtypeStruct((512, 128), F32)
HALF = pltpu.VMEM((PADDED, 512), BF16)
GRANT = pltpu.CompilerParams(vmem_limit_bytes=24 << 20)
SCRATCH = [
    pltpu.VMEM((32, STATES), F32),
    pltpu.VMEM((32, PADDED), F32),
    pltpu.VMEM((32, PADDED), F32),
]
TABLES = [pltpu.VMEM((24, 128), jnp.int32), pltpu.VMEM((16, 128), jnp.int32)]
PLAIN = pltpu.VMEM((512, 128), F32)


def in_hbm(array):
    return pltpu.with_memory_space_constraint(array, pltpu.HBM)


def exchange(amplitudes):
    return lax.all_to_all(amplitudes, ("narrow", "wide"), split_axis=0, concat_axis=0, tiled=True)


def shards(wavefunction, propagator, gate_orders, sector_order, bond_level):
    length = (PROP_ROWS - 1) * 128
    spare = PROP_ROWS * 128 - propagator.shape[0]
    tail = lax.pad(propagator, jnp.float32(0), [(-length, spare, 0)]).reshape(1, 128)
    amplitudes, hi, lo, pull, push = pl.pallas_call(
        first_kernel,
        out_shape=(
            AMPLITUDES,
            HALF,
            HALF,
            jax.ShapeDtypeStruct((4, 24, 128), jnp.int32),
            jax.ShapeDtypeStruct((4, 16, 128), jnp.int32),
        ),
        in_specs=[SMEM, SMEM, HBM, HBM, VMEM, HBM],
        out_specs=(VMEM,) * 5,
        scratch_shapes=[
            pltpu.VMEM((PROP_ROWS, 128), F32),
            pltpu.VMEM((4 * PADDED, 128), F32),
            pltpu.VMEM((16, 128), jnp.int32),
            PLAIN,
            pltpu.VMEM((24, 128), jnp.int32),
            pltpu.VMEM((16, 128), jnp.int32),
            *SCRATCH,
            *TABLES,
            PLAIN,
            pltpu.SemaphoreType.DMA((3,)),
        ],
        compiler_params=GRANT,
        name="first",
    )(
        gate_orders,
        bond_level,
        in_hbm(sector_order.reshape(16, 128)),
        in_hbm(wavefunction.reshape(512, 128)),
        tail,
        in_hbm(propagator),
    )
    amplitudes = exchange(amplitudes)
    amplitudes = pl.pallas_call(
        second_kernel,
        out_shape=AMPLITUDES,
        in_specs=[VMEM] * 5,
        out_specs=VMEM,
        scratch_shapes=SCRATCH,
        compiler_params=GRANT,
        name="second",
    )(amplitudes, pull, push, hi, lo)
    amplitudes = exchange(amplitudes)
    amplitudes = pl.pallas_call(
        third_kernel,
        out_shape=AMPLITUDES,
        in_specs=[VMEM] * 5,
        out_specs=VMEM,
        scratch_shapes=[*SCRATCH, PLAIN],
        compiler_params=GRANT,
        name="third",
    )(amplitudes, pull, push, hi, lo)
    return amplitudes.reshape(-1)


def solution(mesh):
    in_specs = (P(("wide", "narrow")), P(), P(), P(), P())
    out_specs = P(("wide", "narrow"))
    return jax.shard_map(shards, mesh=mesh, in_specs=in_specs, out_specs=out_specs, check_vma=False)
```
